256 devices in a mesh: row: 16 (over x, z_hi, core), col: 16 (over y, z_lo).
Axes of the slice: x: 4, y: 4, z: 8 (z_hi: 2, z_lo: 4; z = z_hi * 4 + z_lo), core: 2. Of those that a mesh axis runs over, the one named last changes fastest.
Arguments:
- amplitudes: bfloat16 [16, 16, 768, 768], P('row', 'col'), may hold values from -0.59765625 to 0.59765625
- ints: bfloat16 [16, 768, 2304], P('row', None, 'col'), may hold values from -0.3984375 to 0.3984375
- eps_occ: float32 [16], replicated, may hold values from -2 to -0.5
- eps_vir: float32 [768], replicated, may hold values from 0.2 to 3
- fock_vir: bfloat16 [768, 768], replicated, may hold values from -2 to 2, as said below
Outputs:
- updated: bfloat16 [16, 16, 768, 768], P('row', 'col')
The draws below stay inside these ranges and needn't reach their ends.
Inputs may be any that keep to these rules, and one draw needn't show every extreme that they name: fock_vir is zero on its diagonal.
All inputs are finite; a program needn't handle non-finite values.
Results may differ from the reference program's by a relative error of at most 0.019.
Values may be sent and summed in bfloat16 or wider, within the bound.
A program may use at most 64 MiB of HBM per device.

```python
import jax
import jax.numpy as jnp
from jax import lax

V = 768
NAUX = 2304
O = 16


def draw_fock_vir(key, part):
    own_key = jax.random.fold_in(key, 7301)
    spread = 1.0 / jnp.sqrt(jnp.float32(V // 16))
    limit = jnp.minimum(jnp.float32(2.0), 6.0 * spread)
    values = jax.random.normal(own_key, (V, V), jnp.float32) * spread
    values = jnp.clip(values, -limit, limit)
    off_diag = 1.0 - jnp.eye(V, dtype=jnp.float32)
    return (values * off_diag).astype(jnp.bfloat16)


def block_levels(stream_key, shape, pieces, low, top_value):
    gain, own = 1.0, jax.random.fold_in(stream_key, 6)
    for position, blocks in pieces:
        heights = jnp.exp(jax.random.uniform(jax.random.fold_in(own, position), (blocks,), jnp.float32, low / len(pieces), top_value / len(pieces)))
        gain = gain * jnp.repeat(heights, shape[position] // blocks).reshape([-1 if axis == position else 1 for axis in range(len(shape))])
    return gain


def normal_values(key, extent, deviation, bound, shards=(), kind=jnp.bfloat16):
    factor_of = block_levels(key, extent, shards, -0.22, 0.18) if shards else 1.0
    array = jax.random.normal(key, extent, jnp.float32) * deviation * factor_of
    return jnp.minimum(jnp.maximum(array, -bound), bound).astype(kind)


def setup_inputs(seed: int = 0) -> dict:
    arg_keys = jax.random.split(jax.random.key(seed), 6)
    return {
        "amplitudes": normal_values(arg_keys[0], (O, O, V, V), 0.1, 0.59765625, ((0, 16), (1, 16))),
        "ints": normal_values(arg_keys[1], (O, V, NAUX), 0.066, 0.3984375, ((0, 16), (2, 16))),
        "eps_occ": jnp.clip(jax.random.uniform(arg_keys[2], (O,), jnp.float32, -2.0, -0.5), -2.0, -0.5),
        "eps_vir": jnp.clip(jax.random.uniform(arg_keys[3], (V,), jnp.float32, 0.2, 3.0), 0.2, 3.0),
        "fock_vir": draw_fock_vir(jax.random.fold_in(arg_keys[5], 71), 0),
    }


def reference(amplitudes, ints, eps_occ, eps_vir, fock_vir):
    occ = ints.shape[0]
    vir = ints.shape[1]
    aux = ints.shape[2]
    flat_ints = ints.reshape(occ * vir, aux)

    def one_column(column):
        amp_col = lax.dynamic_index_in_dim(amplitudes, column, 1, keepdims=False)
        flat_amp = amp_col.reshape(occ * vir, vir)
        cross = jnp.dot(flat_amp.T, flat_ints, preferred_element_type=jnp.float32)
        own = lax.dynamic_index_in_dim(ints, column, 0, keepdims=False)
        dressed = (own.astype(jnp.float32) + cross).astype(jnp.bfloat16)
        pair = jnp.dot(flat_ints, dressed.T, preferred_element_type=jnp.float32).reshape(occ, vir, vir)
        fock_term = jnp.dot(flat_amp, fock_vir, preferred_element_type=jnp.float32).reshape(occ, vir, vir)
        numer = pair + fock_term
        eps_col = lax.dynamic_index_in_dim(eps_occ, column, 0, keepdims=False)
        denom = eps_vir[None, :, None] + eps_vir[None, None, :] - eps_occ[:, None, None] - eps_col
        return (amp_col.astype(jnp.float32) - numer / denom).astype(jnp.bfloat16)

    columns = lax.map(one_column, jnp.arange(occ, dtype=jnp.int32))
    return jnp.transpose(columns, (1, 0, 2, 3))
```

```python
import functools

import jax
import jax.numpy as jnp
from jax import lax
from jax.experimental import pallas as pl
from jax.experimental.pallas import tpu as pltpu
from jax.sharding import Mesh
from jax.sharding import PartitionSpec as P

COL = ("y", "zl")
ROW = ("x", "zh", "core")
STAGES = 4
MESH = pl.DeviceIdType.MESH
BF = jnp.bfloat16
F32 = jnp.float32


def kernel(
    ints, amp, fock, eps_occ, eps_vir, out,
    gath, ampv, fockv, acc, rden,
    give, take, part, x1s, x1r, x2s, x2r, zs, zr, dres,
    stage_out,
    in_sem, out_sem, send_sem, ra, rcore, rx1, rx2, rz, rd,
):
    depth = ints.shape[0]
    vir = ints.shape[1]
    half = vir // 2
    cut = (depth // 2 + 15) // 16 * 16
    x, zh, p = lax.axis_index("x"), lax.axis_index("zh"), lax.axis_index("core")
    y, zl = lax.axis_index("y"), lax.axis_index("zl")
    side = zl // 2
    m = zl + side * (3 - 2 * zl)
    dz = 1 - 2 * side
    rows = [m, 1 - m, 2, 3]
    rows = [v + side * (3 - 2 * v) for v in rows]
    yu, yd, yo = lax.rem(y + 1, 4), lax.rem(y + 3, 4), lax.rem(y + 2, 4)
    xu, xd, xo = lax.rem(x + 1, 4), lax.rem(x + 3, 4), lax.rem(x + 2, 4)
    me = dict(x=x, zh=zh, core=p, y=y, zl=zl)

    def at(**where):
        there = {**me, **where}
        return tuple(there[name] for name in ("x", "zh", "core", "y", "zl"))

    z_plus, z_minus = at(zl=zl + dz), at(zl=zl - dz)
    y_up, y_down = at(y=yu), at(y=yd)
    x_up, x_down = at(x=xu), at(x=xd)
    z_far, mate = at(zh=1 - zh), at(core=1 - p)

    started = []

    def send(src, dst, sem, where):
        copy = pltpu.make_async_remote_copy(
            src_ref=src, dst_ref=dst, send_sem=send_sem.at[len(started)],
            recv_sem=sem, device_id=where, device_id_type=MESH,
        )
        copy.start()
        started.append((copy, None))

    def send_if_inner(src, dst, sem, where):
        copy = pltpu.make_async_remote_copy(
            src_ref=src, dst_ref=dst, send_sem=send_sem.at[len(started)],
            recv_sem=sem, device_id=where, device_id_type=MESH,
        )

        @pl.when(m == 1)
        def _():
            copy.start()

        started.append((copy, m == 1))

    def arrived(dst, sem):
        pltpu.make_async_remote_copy(
            src_ref=dst, dst_ref=dst, send_sem=send_sem.at[0],
            recv_sem=sem, device_id=mate, device_id_type=MESH,
        ).wait_recv()

    own = pltpu.make_async_copy(ints, gath.at[rows[0], y], in_sem.at[0])
    own.start()
    loads = [
        pltpu.make_async_copy(amp.at[:, pl.ds(0, half)], ampv.at[0], in_sem.at[1]),
        pltpu.make_async_copy(amp.at[:, pl.ds(half, half)], ampv.at[1], in_sem.at[2]),
        pltpu.make_async_copy(fock, fockv, in_sem.at[3]),
    ]
    for load in loads:
        load.start()

    barrier = pltpu.get_barrier_semaphore()
    for where in (z_plus, y_up, y_down, x_up, x_down, z_far, mate):
        pl.semaphore_signal(barrier, inc=1, device_id=where, device_id_type=MESH)

    @pl.when(m == 1)
    def _():
        pl.semaphore_signal(barrier, inc=1, device_id=z_minus, device_id_type=MESH)

    own.wait()
    pl.semaphore_wait(barrier, 7 + m)

    lo, hi = pl.ds(0, half), pl.ds(half, half)

    def block(k, q):
        return gath.at[rows[k], q]

    def send_y(k):
        b = block(k, y)
        s = ra.at[rows[k], y]
        send(b.at[:, lo], b.at[:, lo], s.at[0], y_up)
        send(b.at[:, hi], b.at[:, hi], s.at[1], y_down)
        send(b.at[:, hi], b.at[:, hi], s.at[1], y_up)
        send(b.at[:, lo], b.at[:, lo], s.at[0], y_down)

    def start_own():
        b, s = block(0, y), ra.at[rows[0], y, 2]
        send(b, b, s, z_plus)
        send_if_inner(b, b, s, z_minus)
        send_y(0)

    def z_arrive(k):
        b, s = block(k, y), ra.at[rows[k], y, 2]
        arrived(b, s)
        send_if_inner(b, b, s, z_plus if k == 1 else z_minus)

    def y_first(k):
        b, s = block(k, yd), ra.at[rows[k], yd, 0]
        arrived(b.at[:, lo], s)
        send(b.at[:, lo], b.at[:, lo], s, y_up)
        b, s = block(k, yu), ra.at[rows[k], yu, 1]
        arrived(b.at[:, hi], s)
        send(b.at[:, hi], b.at[:, hi], s, y_down)

    def y_second(k):
        b, s = block(k, yd), ra.at[rows[k], yd, 1]
        arrived(b.at[:, hi], s)
        b, s = block(k, yu), ra.at[rows[k], yu, 0]
        arrived(b.at[:, lo], s)

    def y_opposite(k):
        b, s = block(k, yo), ra.at[rows[k], yo]
        arrived(b.at[:, lo], s.at[0])
        arrived(b.at[:, hi], s.at[1])

    mine_term = (x * 4 + zh * 2 + p == y * 4 + zl).astype(jnp.int32).astype(F32)

    def cross(k, q):
        b = block(k, q)

        def columns(h):
            got = jnp.dot(b[...], ampv[h], preferred_element_type=F32)
            return got

        def own_columns(h):
            return jnp.where(h == 0, b[:, :half], b[:, half:]).astype(F32) * mine_term

        give[k, q] = (columns(1 - p) + own_columns(1 - p)).astype(BF)
        send(give.at[k, q], take.at[k, q], rcore.at[k, q], mate)
        part[k, q] = columns(p) + own_columns(p)

    def merge_core(k):
        for q in (yo, yd, yu, y):
            arrived(take.at[k, q], rcore.at[k, q])
        x1s[k] = (part[k, xo] + take[k, xo].astype(F32)).astype(BF)
        send(x1s.at[k, pl.ds(0, cut)], x1r.at[k, pl.ds(0, cut)], rx1.at[k, 0], x_up)
        send(
            x1s.at[k, pl.ds(cut, depth - cut)], x1r.at[k, pl.ds(cut, depth - cut)],
            rx1.at[k, 1], x_down,
        )
        for q in (xu, xd, x):
            part[k, q] += take[k, q].astype(F32)

    def x_relay(k):
        head, tail = pl.ds(0, cut), pl.ds(cut, depth - cut)
        arrived(x1r.at[k, head], rx1.at[k, 0])
        x2s[k, 0, :cut] = (part[k, xu, :cut] + x1r[k, :cut].astype(F32)).astype(BF)
        x2s[k, 0, cut:] = part[k, xu, cut:].astype(BF)
        send(x2s.at[k, 0], x2r.at[k, 0], rx2.at[k, 0], x_up)
        arrived(x1r.at[k, tail], rx1.at[k, 1])
        x2s[k, 1, :cut] = part[k, xd, :cut].astype(BF)
        x2s[k, 1, cut:] = (part[k, xd, cut:] + x1r[k, cut:].astype(F32)).astype(BF)
        send(x2s.at[k, 1], x2r.at[k, 1], rx2.at[k, 1], x_down)

    def x_done(k):
        arrived(x2r.at[k, 0], rx2.at[k, 0])
        arrived(x2r.at[k, 1], rx2.at[k, 1])
        zs[k] = (part[k, x] + (x2r[k, 0].astype(F32) + x2r[k, 1].astype(F32))).astype(BF)
        send(zs.at[k], zr.at[k], rz.at[k], z_far)

    def z_done(k):
        arrived(zr.at[k], rz.at[k])
        dres[k, p, x] = (zs[k].astype(F32) + zr[k].astype(F32)).astype(BF)
        b, s = dres.at[k, p, x], rd.at[k, p, x]
        send(b, b, s.at[0], x_up)
        send(b, b, s.at[0], x_down)
        send(b, b, s.at[0], mate)

    def spread(k):
        head, tail = pl.ds(0, cut), pl.ds(cut, depth - cut)
        b, s = dres.at[k, p, xd], rd.at[k, p, xd]
        arrived(b, s.at[0])
        send(b.at[head], b.at[head], s.at[0], x_up)
        send(b, b, s.at[0], mate)
        b, s = dres.at[k, p, xu], rd.at[k, p, xu]
        arrived(b, s.at[0])
        send(b.at[tail], b.at[tail], s.at[1], x_down)
        send(b, b, s.at[0], mate)

    def spread_far(k):
        head, tail = pl.ds(0, cut), pl.ds(cut, depth - cut)
        b, s = dres.at[k, p, xo], rd.at[k, p, xo]
        arrived(b.at[head], s.at[0])
        arrived(b.at[tail], s.at[1])
        send(b, b, s.at[0], mate)

    def contract(k):
        for q in (x, xd, xu, xo):
            arrived(dres.at[k, 1 - p, q], rd.at[k, 1 - p, q, 0])
        left = gath[rows[k]].reshape(4 * depth, vir)

        @pl.loop(0, 2)
        def _(h):
            right = dres[k, h].reshape(4 * depth, half)
            acc[h] += lax.dot_general(
                left, right, (((0,), (0,)), ((), ())), preferred_element_type=F32
            )

    def early():
        for load in loads:
            load.wait()
        level = eps_occ[x * 4 + zh * 2 + p]
        level2 = eps_occ[y * 4 + zl]
        across = eps_vir[...]
        down = jnp.broadcast_to(across, (128, vir)).T[:, :1]
        for h in range(2):
            f = fockv[:, h * half : (h + 1) * half]
            acc[h] = jnp.dot(ampv[0], f[:half], preferred_element_type=F32) + jnp.dot(
                ampv[1], f[half:], preferred_element_type=F32
            )
            row = across[:, h * half : (h + 1) * half]
            rden[h] = 1.0 / (((down + row) - level) - level2)

    steps = [(0.0, start_own, ()), (0.1, early, ()), (1.0, cross, (0, y))]
    for k in range(STAGES):
        base = 8.1 * k
        if k:
            steps.append((5.4 * k + 1.5, z_arrive, (k,)))
            steps.append((max(5.4 * k + 1.6, 4.3 + 8.1 * (k - 1) + 0.1), send_y, (k,)))
            steps.append((max(5.4 * k + 1.7, 4.3 + 8.1 * (k - 1) + 0.2), cross, (k, y)))
        steps.append((base + 4.3, y_first, (k,)))
        steps.append((base + 7.0, y_second, (k,)))
        steps.append((base + 7.1, cross, (k, yd)))
        steps.append((base + 7.2, cross, (k, yu)))
        done = base + 9.6
        steps.append((done, y_opposite, (k,)))
        steps.append((done + 0.1, cross, (k, yo)))
        steps.append((done + 3.0, merge_core, (k,)))
        steps.append((done + 6.0, x_relay, (k,)))
        steps.append((done + 10.0, x_done, (k,)))
        steps.append((done + 18.0, z_done, (k,)))
        steps.append((done + 22.0, spread, (k,)))
        steps.append((done + 24.0, spread_far, (k,)))
        steps.append((done + 27.0, contract, (k,)))
    for _, step, which in sorted(steps, key=lambda s: s[0]):
        step(*which)

    for h in range(2):
        stage_out[:, h * half : (h + 1) * half] = (
            ampv[h].astype(F32) - acc[h] * rden[h]
        ).astype(BF)
    back = pltpu.make_async_copy(stage_out, out, out_sem)
    back.start()
    for copy, guard in started:
        if guard is None:
            copy.wait_send()
        else:
            pl.when(guard)(copy.wait_send)
    back.wait()


def local(amplitudes, ints, eps_occ, eps_vir, fock_vir):
    vir, depth = ints.shape[1], ints.shape[2]
    half = vir // 2
    anywhere = pl.BlockSpec(memory_space=pl.ANY)
    dma = pltpu.SemaphoreType.DMA
    updated = pl.pallas_call(
        kernel,
        out_shape=jax.ShapeDtypeStruct((vir, vir), BF),
        in_specs=[
            anywhere, anywhere, anywhere,
            pl.BlockSpec(memory_space=pltpu.SMEM),
            pl.BlockSpec(memory_space=pltpu.VMEM),
        ],
        out_specs=anywhere,
        scratch_shapes=[
            pltpu.VMEM((4, 4, depth, vir), BF),
            pltpu.VMEM((2, vir, half), BF),
            pltpu.VMEM((vir, vir), BF),
            pltpu.VMEM((2, vir, half), F32),
            pltpu.VMEM((2, vir, half), F32),
            pltpu.VMEM((STAGES, 4, depth, half), BF),
            pltpu.VMEM((STAGES, 4, depth, half), BF),
            pltpu.VMEM((STAGES, 4, depth, half), F32),
            pltpu.VMEM((STAGES, depth, half), BF),
            pltpu.VMEM((STAGES, depth, half), BF),
            pltpu.VMEM((STAGES, 2, depth, half), BF),
            pltpu.VMEM((STAGES, 2, depth, half), BF),
            pltpu.VMEM((STAGES, depth, half), BF),
            pltpu.VMEM((STAGES, depth, half), BF),
            pltpu.VMEM((STAGES, 2, 4, depth, half), BF),
            pltpu.VMEM((vir, vir), BF),
            dma((4,)), dma, dma((128,)),
            dma((4, 4, 3)), dma((STAGES, 4)), dma((STAGES, 2)), dma((STAGES, 2)),
            dma((STAGES,)), dma((STAGES, 2, 4, 2)),
        ],
        compiler_params=pltpu.CompilerParams(
            collective_id=0, has_side_effects=True, vmem_limit_bytes=60 * 1024 * 1024
        ),
        name="doubles_update",
    )(ints[0].T, amplitudes[0, 0], fock_vir, eps_occ, eps_vir[None, :])
    return updated[None, None]


def solution(mesh):
    torus = Mesh(mesh.devices.reshape(4, 2, 2, 4, 4), ("x", "zh", "core", "y", "zl"))
    placed = (P(ROW, COL, None, None), P(ROW, None, COL), P(), P(), P())
    return jax.shard_map(
        local, mesh=torus, in_specs=placed, out_specs=P(ROW, COL, None, None), check_vma=False
    )
```

```python
import jax
import jax.numpy as jnp
from jax import lax
from jax.experimental import pallas as pl
from jax.experimental.pallas import tpu as pltpu
from jax.sharding import Mesh
from jax.sharding import PartitionSpec as P

COL = ("y", "zl")
ROW = ("x", "zh", "core")
MESH = pl.DeviceIdType.MESH
BF = jnp.bfloat16
F32 = jnp.float32

CHUNKS = (
    (0, 0, 144), (1, 0, 144), (2, 0, 144), (3, 0, 64), (3, 64, 144),
)
ORDER = (
    ("start_own", 0, 0), ("load_wait", 0, 0), ("cross", 0, "y"), ("fock", 0, 0), ("y_first", 0, 0),
    ("z_forward", 1, 0), ("z_forward", 2, 0), ("z_arrive", 1, 0), ("send_y", 1, 0), ("y_second", 0, 0),
    ("cross", 0, "d"), ("cross", 0, "u"), ("cross", 1, "y"), ("y_opposite", 0, 0), ("cross", 0, "o"),
    ("y_first", 1, 0), ("merge_core", 0, 0), ("z_forward", 3, 0), ("z_arrive", 2, 0), ("send_y", 2, 0),
    ("cross", 2, "y"), ("y_second", 1, 0), ("cross", 1, "d"), ("cross", 1, "u"), ("x_relay", 0, 0),
    ("y_opposite", 1, 0), ("cross", 1, "o"), ("y_first", 2, 0), ("z_arrive", 3, 0), ("send_y", 3, 0),
    ("cross", 3, "y"), ("merge_core", 1, 0), ("x_done", 0, 0), ("cross", 4, "y"), ("y_second", 2, 0),
    ("cross", 2, "d"), ("cross", 2, "u"), ("x_relay", 1, 0), ("y_opposite", 2, 0), ("cross", 2, "o"),
    ("y_first", 3, 0), ("send_y", 4, 0), ("y_second", 3, 0), ("cross", 3, "d"), ("cross", 3, "u"),
    ("merge_core", 2, 0), ("x_done", 1, 0), ("y_opposite", 3, 0), ("cross", 3, "o"), ("y_first", 4, 0),
    ("x_relay", 2, 0), ("merge_core", 3, 0), ("y_second", 4, 0), ("cross", 4, "d"), ("cross", 4, "u"),
    ("y_opposite", 4, 0), ("cross", 4, "o"), ("z_done", 0, 0), ("x_done", 2, 0), ("merge_core", 4, 0),
    ("x_relay", 3, 0), ("spread", 0, 0), ("x_relay", 4, 0), ("x_done", 3, 0), ("z_done", 1, 0),
    ("spread_far", 0, 0), ("x_done", 4, 0), ("contract", 0, 0), ("spread", 1, 0), ("z_done", 2, 0),
    ("spread_far", 1, 0), ("z_done", 3, 0), ("contract", 1, 0), ("spread", 2, 0), ("spread", 3, 0),
    ("z_done", 4, 0), ("spread_far", 2, 0), ("spread_far", 3, 0), ("spread", 4, 0), ("contract", 2, 0),
    ("contract", 3, 0), ("spread_far", 4, 0), ("contract", 4, 0),
)


def kernel(
    ints, amp, fock, out,
    gath, ampv, fockv, acc, temp,
    give, take, part, x1s, x1r, x2s, x2r, zs, zr, dres,
    in_sem, out_sem, send_sem, ra, raz, rcore, rx1, rx2, rz, rd,
):
    vir = ints.shape[1]
    half = vir // 2
    x, zh, p = lax.axis_index("x"), lax.axis_index("zh"), lax.axis_index("core")
    y, zl = lax.axis_index("y"), lax.axis_index("zl")
    side = zl // 2
    m = zl + side * (3 - 2 * zl)
    dz = 1 - 2 * side
    rows = [v + side * (3 - 2 * v) for v in (m, 1 - m, 2, 3)]
    yu, yd, yo = lax.rem(y + 1, 4), lax.rem(y + 3, 4), lax.rem(y + 2, 4)
    xu, xd, xo = lax.rem(x + 1, 4), lax.rem(x + 3, 4), lax.rem(x + 2, 4)
    of_y = {"y": y, "u": yu, "d": yd, "o": yo}
    me = dict(x=x, zh=zh, core=p, y=y, zl=zl)

    def at(**where):
        there = {**me, **where}
        return tuple(there[name] for name in ("x", "zh", "core", "y", "zl"))

    z_plus, z_minus = at(zl=zl + dz), at(zl=zl - dz)
    y_up, y_down = at(y=yu), at(y=yd)
    x_up, x_down = at(x=xu), at(x=xd)
    z_far, mate = at(zh=1 - zh), at(core=1 - p)

    started = []

    def send(src, dst, sem, where, guard=None):
        copy = pltpu.make_async_remote_copy(
            src_ref=src, dst_ref=dst, send_sem=send_sem.at[len(started)],
            recv_sem=sem, device_id=where, device_id_type=MESH,
        )
        if guard is None:
            copy.start()
        else:
            pl.when(guard)(copy.start)
        started.append((copy, guard))

    def arrived(dst, sem):
        pltpu.make_async_remote_copy(
            src_ref=dst, dst_ref=dst, send_sem=send_sem.at[0],
            recv_sem=sem, device_id=mate, device_id_type=MESH,
        ).wait_recv()

    own = pltpu.make_async_copy(ints, gath.at[rows[0], y], in_sem.at[0])
    own.start()
    loads = [
        pltpu.make_async_copy(amp.at[:, pl.ds(0, half)], ampv.at[0], in_sem.at[1]),
        pltpu.make_async_copy(amp.at[:, pl.ds(half, half)], ampv.at[1], in_sem.at[2]),
        pltpu.make_async_copy(fock, fockv, in_sem.at[3]),
    ]
    for load in loads:
        load.start()

    barrier = pltpu.get_barrier_semaphore()
    for where in (z_plus, y_up, y_down, x_up, x_down, z_far, mate):
        pl.semaphore_signal(barrier, inc=1, device_id=where, device_id_type=MESH)

    @pl.when(m == 1)
    def _():
        pl.semaphore_signal(barrier, inc=1, device_id=z_minus, device_id_type=MESH)

    own.wait()
    pl.semaphore_wait(barrier, 7 + m)

    lo, hi = pl.ds(0, half), pl.ds(half, half)
    is_mine = x * 4 + zh * 2 + p == y * 4 + zl

    def span(i):
        return CHUNKS[i][1], CHUNKS[i][2]

    def cut(i):
        a, b = span(i)
        middle = a + ((b - a) // 16 + i % 2) // 2 * 16
        return pl.ds(a, middle - a), pl.ds(middle, b - middle)

    def whole(i):
        a, b = span(i)
        return pl.ds(a, b - a)

    def block(i, q):
        return gath.at[rows[CHUNKS[i][0]], q, whole(i)]

    def send_y(i):
        b, s = block(i, y), ra.at[i, y]
        send(b.at[:, lo], b.at[:, lo], s.at[0], y_up)
        send(b.at[:, hi], b.at[:, hi], s.at[1], y_down)
        send(b.at[:, hi], b.at[:, hi], s.at[1], y_up)
        send(b.at[:, lo], b.at[:, lo], s.at[0], y_down)

    def start_own():
        b, s = gath.at[rows[0], y], raz.at[rows[0]]
        send(b, b, s, z_plus)
        send(b, b, s, z_minus, m == 1)
        for i, chunk in enumerate(CHUNKS):
            if chunk[0] == 0:
                send_y(i)

    def z_forward(k):
        b, s = gath.at[rows[k], y], raz.at[rows[k]]
        pl.when(m == 1)(lambda: arrived(b, s))
        send(b, b, s, z_plus if k == 1 else z_minus, m == 1)

    def z_arrive(k):
        b, s = gath.at[rows[k], y], raz.at[rows[k]]
        pl.when(m == 0)(lambda: arrived(b, s))

    def y_first(i):
        b, s = block(i, yd), ra.at[i, yd, 0]
        arrived(b.at[:, lo], s)
        send(b.at[:, lo], b.at[:, lo], s, y_up)
        b, s = block(i, yu), ra.at[i, yu, 1]
        arrived(b.at[:, hi], s)
        send(b.at[:, hi], b.at[:, hi], s, y_down)

    def y_second(i):
        arrived(block(i, yd).at[:, hi], ra.at[i, yd, 1])
        arrived(block(i, yu).at[:, lo], ra.at[i, yu, 0])

    def y_opposite(i):
        arrived(block(i, yo).at[:, lo], ra.at[i, yo, 0])
        arrived(block(i, yo).at[:, hi], ra.at[i, yo, 1])

    def cross(i, which):
        k, (a, b), q = CHUNKS[i][0], span(i), of_y[which]
        left = gath.at[rows[k], q, whole(i)]

        def term(into, h):
            into[...] = jnp.dot(left[...], ampv[h], preferred_element_type=F32)
            for side_of in range(2):

                @pl.when(is_mine & (h == side_of))
                def _(side_of=side_of):
                    into[...] += left[:, side_of * half : (side_of + 1) * half].astype(F32)

        term(temp.at[pl.ds(0, b - a)], 1 - p)
        give[k, q, a:b] = temp[: b - a].astype(BF)
        sent = (k, q, whole(i))
        send(give.at[sent], take.at[sent], rcore.at[i, q], mate)
        term(part.at[k, q, whole(i)], p)

    def merge_core(i):
        k, (a, b) = CHUNKS[i][0], span(i)
        for q in (y, yd, yu, yo):
            arrived(take.at[k, q, whole(i)], rcore.at[i, q])
        x1s[k, a:b] = (part[k, xo, a:b] + take[k, xo, a:b].astype(F32)).astype(BF)
        head, tail = cut(i)
        send(x1s.at[k, head], x1r.at[k, head], rx1.at[i, 0], x_up)
        send(x1s.at[k, tail], x1r.at[k, tail], rx1.at[i, 1], x_down)
        for q in (xu, xd, x):
            part[k, q, a:b] += take[k, q, a:b].astype(F32)

    def x_relay(i):
        k, (a, b) = CHUNKS[i][0], span(i)
        head, tail = cut(i)
        arrived(x1r.at[k, head], rx1.at[i, 0])
        x2s[k, 0, head] = (part[k, xu, head] + x1r[k, head].astype(F32)).astype(BF)
        x2s[k, 0, tail] = part[k, xu, tail].astype(BF)
        send(x2s.at[k, 0, whole(i)], x2r.at[k, 0, whole(i)], rx2.at[i, 0], x_up)
        arrived(x1r.at[k, tail], rx1.at[i, 1])
        x2s[k, 1, head] = part[k, xd, head].astype(BF)
        x2s[k, 1, tail] = (part[k, xd, tail] + x1r[k, tail].astype(F32)).astype(BF)
        send(x2s.at[k, 1, whole(i)], x2r.at[k, 1, whole(i)], rx2.at[i, 1], x_down)

    def x_done(i):
        k, (a, b) = CHUNKS[i][0], span(i)
        arrived(x2r.at[k, 0, whole(i)], rx2.at[i, 0])
        arrived(x2r.at[k, 1, whole(i)], rx2.at[i, 1])
        both = x2r[k, 0, a:b].astype(F32) + x2r[k, 1, a:b].astype(F32)
        zs[k, a:b] = (part[k, x, a:b] + both).astype(BF)
        send(zs.at[k, whole(i)], zr.at[k, whole(i)], rz.at[i], z_far)

    def z_done(i):
        k, (a, b) = CHUNKS[i][0], span(i)
        arrived(zr.at[k, whole(i)], rz.at[i])
        dres[k, p, x, a:b] = (zs[k, a:b].astype(F32) + zr[k, a:b].astype(F32)).astype(BF)
        b, s = dres.at[k, p, x, whole(i)], rd.at[i, p, x]
        send(b, b, s.at[0], x_up)
        send(b, b, s.at[0], x_down)
        send(b, b, s.at[0], mate)

    def spread(i):
        k = CHUNKS[i][0]
        head, tail = cut(i)
        for q, piece, sem, where in ((xd, head, 0, x_up), (xu, tail, 1, x_down)):
            b, s = dres.at[k, p, q, whole(i)], rd.at[i, p, q]
            arrived(b, s.at[0])
            c = dres.at[k, p, q, piece]
            send(c, c, s.at[sem], where)
            send(b, b, s.at[0], mate)

    def spread_far(i):
        k = CHUNKS[i][0]
        head, tail = cut(i)
        arrived(dres.at[k, p, xo, head], rd.at[i, p, xo, 0])
        arrived(dres.at[k, p, xo, tail], rd.at[i, p, xo, 1])
        b = dres.at[k, p, xo, whole(i)]
        send(b, b, rd.at[i, p, xo, 0], mate)

    def put(h):
        return pltpu.make_async_copy(
            acc.at[pl.ds(h * half, half)], out.at[pl.ds(h * half, half)], out_sem.at[h]
        )

    def contract(i):
        k, (a, b) = CHUNKS[i][0], span(i)
        for q in (x, xd, xu, xo):
            arrived(dres.at[k, 1 - p, q, whole(i)], rd.at[i, 1 - p, q, 0])
        left = gath[rows[k], :, a:b].reshape(4 * (b - a), vir)
        right = jnp.concatenate(
            [dres[k, h, :, a:b].reshape(4 * (b - a), half) for h in range(2)], axis=-1
        )
        last = ORDER[-1] == ("contract", i, 0)
        for h in range(2):
            r = slice(h * half, (h + 1) * half)
            acc[r] += lax.dot_general(
                left[:, r], right, (((0,), (0,)), ((), ())), preferred_element_type=F32
            )
            if last:
                put(h).start()

    def load_wait():
        for load in loads:
            load.wait()

    def fock_term():
        acc[...] = jnp.dot(ampv[0], fockv[:half], preferred_element_type=F32) + jnp.dot(
            ampv[1], fockv[half:], preferred_element_type=F32
        )

    for name, i, which in ORDER:
        if name == "cross":
            cross(i, which)
        elif name == "start_own":
            start_own()
        elif name == "load_wait":
            load_wait()
        elif name == "fock":
            fock_term()
        else:
            {
                "z_arrive": z_arrive, "z_forward": z_forward, "send_y": send_y, "y_first": y_first,
                "y_second": y_second, "y_opposite": y_opposite, "merge_core": merge_core,
                "x_relay": x_relay, "x_done": x_done, "z_done": z_done, "spread": spread,
                "spread_far": spread_far, "contract": contract,
            }[name](i)

    for copy, guard in started:
        if guard is None:
            copy.wait_send()
        else:
            pl.when(guard)(copy.wait_send)
    for h in range(2):
        put(h).wait()


def local(amplitudes, ints, eps_occ, eps_vir, fock_vir):
    vir, depth = ints.shape[1], ints.shape[2]
    half = vir // 2
    n = len(CHUNKS)
    anywhere = pl.BlockSpec(memory_space=pl.ANY)
    dma = pltpu.SemaphoreType.DMA
    numer = pl.pallas_call(
        kernel,
        out_shape=jax.ShapeDtypeStruct((vir, vir), F32),
        in_specs=[anywhere] * 3,
        out_specs=anywhere,
        scratch_shapes=[
            pltpu.VMEM((4, 4, depth, vir), BF),
            pltpu.VMEM((2, vir, half), BF),
            pltpu.VMEM((vir, vir), BF),
            pltpu.VMEM((vir, vir), F32),
            pltpu.VMEM((depth, half), F32),
            pltpu.VMEM((4, 4, depth, half), BF),
            pltpu.VMEM((4, 4, depth, half), BF),
            pltpu.VMEM((4, 4, depth, half), F32),
            pltpu.VMEM((4, depth, half), BF),
            pltpu.VMEM((4, depth, half), BF),
            pltpu.VMEM((4, 2, depth, half), BF),
            pltpu.VMEM((4, 2, depth, half), BF),
            pltpu.VMEM((4, depth, half), BF),
            pltpu.VMEM((4, depth, half), BF),
            pltpu.VMEM((4, 2, 4, depth, half), BF),
            dma((4,)), dma((2,)), dma((5 + 23 * n,)),
            dma((n, 4, 2)), dma((4,)), dma((n, 4)), dma((n, 2)), dma((n, 2)),
            dma((n,)), dma((n, 2, 4, 2)),
        ],
        compiler_params=pltpu.CompilerParams(
            collective_id=0, has_side_effects=True, vmem_limit_bytes=60 * 1024 * 1024
        ),
        name="doubles_numerator",
    )(ints[0].T, amplitudes[0, 0], fock_vir)
    level = eps_occ[lax.axis_index(ROW)]
    level2 = eps_occ[lax.axis_index(COL)]
    denom = eps_vir[:, None] + eps_vir[None, :] - level - level2
    updated = (amplitudes[0, 0].astype(F32) - numer / denom).astype(BF)
    return updated[None, None]


def solution(mesh):
    torus = Mesh(mesh.devices.reshape(4, 2, 2, 4, 4), ("x", "zh", "core", "y", "zl"))
    placed = (P(ROW, COL, None, None), P(ROW, None, COL), P(), P(), P())
    return jax.shard_map(
        local, mesh=torus, in_specs=placed, out_specs=P(ROW, COL, None, None), check_vma=False
    )
```

```python
import jax
import jax.numpy as jnp
from jax import lax
from jax.experimental import pallas as pl
from jax.experimental.pallas import tpu as pltpu
from jax.sharding import Mesh
from jax.sharding import PartitionSpec as P

COL = ("y", "zl")
ROW = ("x", "zh", "core")
MESH = pl.DeviceIdType.MESH
BF = jnp.bfloat16
F32 = jnp.float32

CHUNKS = (
    (0, 0, 144), (1, 0, 144), (2, 0, 144), (3, 0, 64), (3, 64, 144),
)
PIECES = (
    (0, 0, 144), (1, 0, 144), (2, 0, 144), (3, 0, 64), (3, 64, 144),
)
ORDER = (
    ("start_own", 0, 0), ("load_wait", 0, 0), ("fock", 0, 0), ("y_first", 0, 0), ("z_forward", 1, 0),
    ("y_second", 0, 0), ("z_forward", 2, 0), ("z_arrive", 1, 0), ("cross", 0, "d"), ("send_y", 1, 0),
    ("y_opposite", 0, 0), ("cross", 0, "o"), ("cross", 1, "y"), ("cross", 0, "y"), ("cross", 0, "u"),
    ("y_first", 1, 0), ("z_forward", 3, 0), ("z_arrive", 2, 0), ("merge_core", 0, 0), ("send_y", 2, 0),
    ("y_second", 1, 0), ("x_relay", 0, 0), ("cross", 1, "d"), ("y_first", 2, 0), ("z_arrive", 3, 0),
    ("y_opposite", 1, 0), ("cross", 1, "o"), ("cross", 1, "u"), ("x_done", 0, 0), ("cross", 2, "y"),
    ("merge_core", 1, 0), ("y_second", 2, 0), ("send_y", 3, 0), ("cross", 2, "u"), ("rden", 0, 0),
    ("cross", 4, "y"), ("y_opposite", 2, 0), ("y_first", 3, 0), ("x_relay", 1, 0), ("cross", 2, "o"),
    ("cross", 2, "d"), ("cross", 3, "y"), ("merge_core", 2, 0), ("y_second", 3, 0), ("send_y", 4, 0),
    ("y_opposite", 3, 0), ("z_done", 0, 0), ("cross", 3, "o"), ("cross", 3, "d"), ("x_done", 1, 0),
    ("y_first", 4, 0), ("x_relay", 2, 0), ("cross", 3, "u"), ("spread", 0, 0), ("merge_core", 3, 0),
    ("y_opposite", 4, 0), ("cross", 4, "o"), ("y_second", 4, 0), ("cross", 4, "u"), ("cross", 4, "d"),
    ("x_done", 2, 0), ("merge_core", 4, 0), ("x_relay", 3, 0), ("z_done", 1, 0), ("x_relay", 4, 0),
    ("x_done", 3, 0), ("spread_far", 0, 0), ("z_done", 2, 0), ("spread", 1, 0), ("x_done", 4, 0),
    ("z_done", 3, 0), ("spread_far", 1, 0), ("spread", 2, 0), ("contract", 0, 0), ("z_done", 4, 0),
    ("contract", 1, 0), ("spread", 3, 0), ("spread_far", 2, 0), ("spread", 4, 0), ("spread_far", 3, 0),
    ("contract", 2, 0), ("spread_far", 4, 0), ("contract", 3, 0), ("contract", 4, 0),
)


def kernel(
    ints, amp, fock, eps_occ, eps_vir, out,
    gath, ampv, fockv, acc, temp, rden, done, occs, virs,
    give, take, part, x1s, x1r, x2s, x2r, zs, zr, dres,
    in_sem, out_sem, send_sem, ra, raz, rcore, rx1, rx2, rz, rd,
):
    vir = ints.shape[1]
    half = vir // 2
    x, zh, p = lax.axis_index("x"), lax.axis_index("zh"), lax.axis_index("core")
    y, zl = lax.axis_index("y"), lax.axis_index("zl")
    side = zl // 2
    m = zl + side * (3 - 2 * zl)
    dz = 1 - 2 * side
    rows = [v + side * (3 - 2 * v) for v in (m, 1 - m, 2, 3)]
    yu, yd, yo = lax.rem(y + 1, 4), lax.rem(y + 3, 4), lax.rem(y + 2, 4)
    xu, xd, xo = lax.rem(x + 1, 4), lax.rem(x + 3, 4), lax.rem(x + 2, 4)
    of_y = {"y": y, "u": yu, "d": yd, "o": yo}
    me = dict(x=x, zh=zh, core=p, y=y, zl=zl)

    def at(**where):
        there = {**me, **where}
        return tuple(there[name] for name in ("x", "zh", "core", "y", "zl"))

    z_plus, z_minus = at(zl=zl + dz), at(zl=zl - dz)
    y_up, y_down = at(y=yu), at(y=yd)
    x_up, x_down = at(x=xu), at(x=xd)
    z_far, mate = at(zh=1 - zh), at(core=1 - p)

    started = []

    def send(src, dst, sem, where, guard=None):
        copy = pltpu.make_async_remote_copy(
            src_ref=src, dst_ref=dst, send_sem=send_sem.at[len(started)],
            recv_sem=sem, device_id=where, device_id_type=MESH,
        )
        if guard is None:
            copy.start()
        else:
            pl.when(guard)(copy.start)
        started.append((copy, guard))

    def arrived(dst, sem):
        pltpu.make_async_remote_copy(
            src_ref=dst, dst_ref=dst, send_sem=send_sem.at[0],
            recv_sem=sem, device_id=mate, device_id_type=MESH,
        ).wait_recv()

    own = pltpu.make_async_copy(ints, gath.at[rows[0], y], in_sem.at[0])
    own.start()
    loads = [
        pltpu.make_async_copy(amp.at[:, pl.ds(0, half)], ampv.at[0], in_sem.at[1]),
        pltpu.make_async_copy(amp.at[:, pl.ds(half, half)], ampv.at[1], in_sem.at[2]),
        pltpu.make_async_copy(fock, fockv, in_sem.at[3]),
        pltpu.make_async_copy(eps_occ, occs, in_sem.at[4]),
        pltpu.make_async_copy(eps_vir, virs, in_sem.at[5]),
    ]
    for load in loads:
        load.start()

    barrier = pltpu.get_barrier_semaphore()
    for where in (z_plus, y_up, y_down, x_up, x_down, z_far, mate):
        pl.semaphore_signal(barrier, inc=1, device_id=where, device_id_type=MESH)

    @pl.when(m == 1)
    def _():
        pl.semaphore_signal(barrier, inc=1, device_id=z_minus, device_id_type=MESH)

    own.wait()
    pl.semaphore_wait(barrier, 7 + m)

    lo, hi = pl.ds(0, half), pl.ds(half, half)
    is_mine = x * 4 + zh * 2 + p == y * 4 + zl

    def span(i, table=CHUNKS):
        return table[i][1], table[i][2]

    def cut(i, table=CHUNKS):
        a, b = span(i, table)
        middle = a + ((b - a) // 16 + i % 2) // 2 * 16
        return pl.ds(a, middle - a), pl.ds(middle, b - middle)

    def whole(i, table=CHUNKS):
        a, b = span(i, table)
        return pl.ds(a, b - a)

    def block(i, q):
        return gath.at[rows[CHUNKS[i][0]], q, whole(i)]

    def send_y(i):
        b, s = block(i, y), ra.at[i, y]
        send(b.at[:, lo], b.at[:, lo], s.at[0], y_up)
        send(b.at[:, hi], b.at[:, hi], s.at[1], y_down)
        send(b.at[:, hi], b.at[:, hi], s.at[1], y_up)
        send(b.at[:, lo], b.at[:, lo], s.at[0], y_down)

    def start_own():
        b, s = gath.at[rows[0], y], raz.at[rows[0]]
        send(b, b, s, z_plus)
        send(b, b, s, z_minus, m == 1)
        for i, chunk in enumerate(CHUNKS):
            if chunk[0] == 0:
                send_y(i)

    def z_forward(k):
        b, s = gath.at[rows[k], y], raz.at[rows[k]]
        pl.when(m == 1)(lambda: arrived(b, s))
        send(b, b, s, z_plus if k == 1 else z_minus, m == 1)

    def z_arrive(k):
        b, s = gath.at[rows[k], y], raz.at[rows[k]]
        pl.when(m == 0)(lambda: arrived(b, s))

    def y_first(i):
        b, s = block(i, yd), ra.at[i, yd, 0]
        arrived(b.at[:, lo], s)
        send(b.at[:, lo], b.at[:, lo], s, y_up)
        b, s = block(i, yu), ra.at[i, yu, 1]
        arrived(b.at[:, hi], s)
        send(b.at[:, hi], b.at[:, hi], s, y_down)

    def y_second(i):
        arrived(block(i, yd).at[:, hi], ra.at[i, yd, 1])
        arrived(block(i, yu).at[:, lo], ra.at[i, yu, 0])

    def y_opposite(i):
        arrived(block(i, yo).at[:, lo], ra.at[i, yo, 0])
        arrived(block(i, yo).at[:, hi], ra.at[i, yo, 1])

    def cross(i, which):
        k, (a, b), q = CHUNKS[i][0], span(i), of_y[which]
        left = gath.at[rows[k], q, whole(i)]

        def term(into, h):
            into[...] = jnp.dot(left[...], ampv[h], preferred_element_type=F32)
            for side_of in range(2):

                @pl.when(is_mine & (h == side_of))
                def _(side_of=side_of):
                    into[...] += left[:, side_of * half : (side_of + 1) * half].astype(F32)

        term(temp.at[pl.ds(0, b - a)], 1 - p)
        give[k, q, a:b] = temp[: b - a].astype(BF)
        sent = (k, q, whole(i))
        send(give.at[sent], take.at[sent], rcore.at[i, q], mate)
        term(part.at[k, q, whole(i)], p)

    def merge_core(i):
        k, (a, b) = CHUNKS[i][0], span(i)
        for q in (y, yd, yu, yo):
            arrived(take.at[k, q, whole(i)], rcore.at[i, q])
        x1s[k, a:b] = (part[k, xo, a:b] + take[k, xo, a:b].astype(F32)).astype(BF)
        head, tail = cut(i)
        send(x1s.at[k, head], x1r.at[k, head], rx1.at[i, 0], x_up)
        send(x1s.at[k, tail], x1r.at[k, tail], rx1.at[i, 1], x_down)
        for q in (xu, xd, x):
            part[k, q, a:b] += take[k, q, a:b].astype(F32)

    def x_relay(i):
        k, (a, b) = CHUNKS[i][0], span(i)
        head, tail = cut(i)
        arrived(x1r.at[k, head], rx1.at[i, 0])
        x2s[k, 0, head] = (part[k, xu, head] + x1r[k, head].astype(F32)).astype(BF)
        x2s[k, 0, tail] = part[k, xu, tail].astype(BF)
        send(x2s.at[k, 0, whole(i)], x2r.at[k, 0, whole(i)], rx2.at[i, 0], x_up)
        arrived(x1r.at[k, tail], rx1.at[i, 1])
        x2s[k, 1, head] = part[k, xd, head].astype(BF)
        x2s[k, 1, tail] = (part[k, xd, tail] + x1r[k, tail].astype(F32)).astype(BF)
        send(x2s.at[k, 1, whole(i)], x2r.at[k, 1, whole(i)], rx2.at[i, 1], x_down)

    def x_done(i):
        k, (a, b) = CHUNKS[i][0], span(i)
        arrived(x2r.at[k, 0, whole(i)], rx2.at[i, 0])
        arrived(x2r.at[k, 1, whole(i)], rx2.at[i, 1])
        both = x2r[k, 0, a:b].astype(F32) + x2r[k, 1, a:b].astype(F32)
        zs[k, a:b] = (part[k, x, a:b] + both).astype(BF)
        for c, (of, first, last) in enumerate(PIECES):
            if of == k and a <= first and last <= b:
                r = whole(c, PIECES)
                send(zs.at[k, r], zr.at[k, r], rz.at[c], z_far)

    def z_done(i):
        k, (a, b) = PIECES[i][0], span(i, PIECES)
        arrived(zr.at[k, whole(i, PIECES)], rz.at[i])
        dres[k, p, x, a:b] = (zs[k, a:b].astype(F32) + zr[k, a:b].astype(F32)).astype(BF)
        b, s = dres.at[k, p, x, whole(i, PIECES)], rd.at[i, p, x]
        send(b, b, s.at[0], x_up)
        send(b, b, s.at[0], x_down)
        send(b, b, s.at[0], mate)

    def spread(i):
        k = PIECES[i][0]
        head, tail = cut(i, PIECES)
        for q, piece, sem, where in ((xd, head, 0, x_up), (xu, tail, 1, x_down)):
            b, s = dres.at[k, p, q, whole(i, PIECES)], rd.at[i, p, q]
            arrived(b, s.at[0])
            c = dres.at[k, p, q, piece]
            send(c, c, s.at[sem], where)
            send(b, b, s.at[0], mate)

    def spread_far(i):
        k = PIECES[i][0]
        head, tail = cut(i, PIECES)
        arrived(dres.at[k, p, xo, head], rd.at[i, p, xo, 0])
        arrived(dres.at[k, p, xo, tail], rd.at[i, p, xo, 1])
        b = dres.at[k, p, xo, whole(i, PIECES)]
        send(b, b, rd.at[i, p, xo, 0], mate)

    def put(h):
        return pltpu.make_async_copy(
            done.at[pl.ds(h * half, half)], out.at[pl.ds(h * half, half)], out_sem.at[h]
        )

    def contract(i):
        k, (a, b) = PIECES[i][0], span(i, PIECES)
        for q in (x, xd, xu, xo):
            arrived(dres.at[k, 1 - p, q, whole(i, PIECES)], rd.at[i, 1 - p, q, 0])
        left = gath[rows[k], :, a:b].reshape(4 * (b - a), vir)
        right = jnp.concatenate(
            [dres[k, h, :, a:b].reshape(4 * (b - a), half) for h in range(2)], axis=-1
        )
        last = ORDER[-1] == ("contract", i, 0)
        for h in range(2):
            r = slice(h * half, (h + 1) * half)
            term = lax.dot_general(
                left[:, r], right, (((0,), (0,)), ((), ())), preferred_element_type=F32
            )
            if last:
                change = (acc[r] + term) * rden[r]
                for c in range(2):
                    cols = slice(c * half, (c + 1) * half)
                    done[r, cols] = (ampv[c, r].astype(F32) - change[:, cols]).astype(BF)
                put(h).start()
            else:
                acc[r] += term

    def load_wait():
        for load in loads:
            load.wait()

    def fock_term():
        acc[...] = jnp.dot(ampv[0], fockv[:half], preferred_element_type=F32) + jnp.dot(
            ampv[1], fockv[half:], preferred_element_type=F32
        )

    def denominators():
        level = occs[x * 4 + zh * 2 + p]
        level2 = occs[y * 4 + zl]
        across = virs[...].reshape(1, vir)
        down = jnp.broadcast_to(across, (128, vir)).T[:, :1]
        rden[...] = 1.0 / (((down + across) - level) - level2)

    for name, i, which in ORDER:
        if name == "cross":
            cross(i, which)
        elif name == "start_own":
            start_own()
        elif name == "load_wait":
            load_wait()
        elif name == "fock":
            fock_term()
        elif name == "rden":
            denominators()
        else:
            {
                "z_arrive": z_arrive, "z_forward": z_forward, "send_y": send_y, "y_first": y_first,
                "y_second": y_second, "y_opposite": y_opposite, "merge_core": merge_core,
                "x_relay": x_relay, "x_done": x_done, "z_done": z_done, "spread": spread,
                "spread_far": spread_far, "contract": contract,
            }[name](i)

    for copy, guard in started:
        if guard is None:
            copy.wait_send()
        else:
            pl.when(guard)(copy.wait_send)
    for h in range(2):
        put(h).wait()


def local(amplitudes, ints, eps_occ, eps_vir, fock_vir):
    vir, depth = ints.shape[1], ints.shape[2]
    half = vir // 2
    n, n2 = len(CHUNKS), len(PIECES)
    anywhere = pl.BlockSpec(memory_space=pl.ANY)
    dma = pltpu.SemaphoreType.DMA
    updated = pl.pallas_call(
        kernel,
        out_shape=jax.ShapeDtypeStruct((vir, vir), BF),
        in_specs=[anywhere] * 5,
        out_specs=anywhere,
        scratch_shapes=[
            pltpu.VMEM((4, 4, depth, vir), BF),
            pltpu.VMEM((2, vir, half), BF),
            pltpu.VMEM((vir, vir), BF),
            pltpu.VMEM((vir, vir), F32),
            pltpu.VMEM((depth, half), F32),
            pltpu.VMEM((vir, vir), F32),
            pltpu.VMEM((vir, vir), BF),
            pltpu.SMEM(eps_occ.shape, F32),
            pltpu.VMEM((vir,), F32),
            pltpu.VMEM((4, 4, depth, half), BF),
            pltpu.VMEM((4, 4, depth, half), BF),
            pltpu.VMEM((4, 4, depth, half), F32),
            pltpu.VMEM((4, depth, half), BF),
            pltpu.VMEM((4, depth, half), BF),
            pltpu.VMEM((4, 2, depth, half), BF),
            pltpu.VMEM((4, 2, depth, half), BF),
            pltpu.VMEM((4, depth, half), BF),
            pltpu.VMEM((4, depth, half), BF),
            pltpu.VMEM((4, 2, 4, depth, half), BF),
            dma((6,)), dma((2,)), dma((5 + 14 * n + 9 * n2,)),
            dma((n, 4, 2)), dma((4,)), dma((n, 4)), dma((n, 2)), dma((n, 2)),
            dma((n2,)), dma((n2, 2, 4, 2)),
        ],
        compiler_params=pltpu.CompilerParams(
            collective_id=0, has_side_effects=True, vmem_limit_bytes=60 * 1024 * 1024
        ),
        name="doubles_update",
    )(ints[0].T, amplitudes[0, 0], fock_vir, eps_occ, eps_vir)
    return updated[None, None]


def solution(mesh):
    torus = Mesh(mesh.devices.reshape(4, 2, 2, 4, 4), ("x", "zh", "core", "y", "zl"))
    placed = (P(ROW, COL, None, None), P(ROW, None, COL), P(), P(), P())
    return jax.shard_map(
        local, mesh=torus, in_specs=placed, out_specs=P(ROW, COL, None, None), check_vma=False
    )
```

```python
import jax
import jax.numpy as jnp
from jax import lax
from jax.experimental import pallas as pl
from jax.experimental.pallas import tpu as pltpu
from jax.sharding import Mesh
from jax.sharding import PartitionSpec as P

COL = ("y", "zl")
ROW = ("x", "zh", "core")
MESH = pl.DeviceIdType.MESH
BF = jnp.bfloat16
F32 = jnp.float32

CHUNKS = (
    (0, 0, 144), (1, 0, 144), (2, 0, 144), (3, 0, 144),
)
PIECES = (
    (0, 0, 144), (1, 0, 144), (2, 0, 144), (3, 0, 144),
)
ORDER = (
    ("start_own", 0, 0), ("y_first", 0, 0), ("z_forward", 1, 0), ("load_wait", 0, 0), ("cross", 0, "y"),
    ("z_arrive", 1, 0), ("z_forward", 2, 0), ("send_y", 1, 0), ("cross", 1, "y"), ("fock", 0, 0),
    ("y_first", 1, 0), ("z_arrive", 2, 0), ("y_opposite", 0, 0), ("cross", 0, "o"), ("y_second", 1, 0),
    ("y_second", 0, 0), ("z_forward", 3, 0), ("send_y", 2, 0), ("cross", 1, "u"), ("cross", 0, "d"),
    ("cross", 0, "u"), ("cross", 1, "d"), ("merge_core", 0, 0), ("y_opposite", 1, 0), ("cross", 1, "o"),
    ("y_first", 2, 0), ("z_arrive", 3, 0), ("x_relay", 0, 0), ("y_second", 2, 0), ("cross", 2, "d"),
    ("merge_core", 1, 0), ("cross", 2, "y"), ("send_y", 3, 0), ("y_opposite", 2, 0), ("cross", 2, "o"),
    ("x_relay", 1, 0), ("cross", 2, "u"), ("x_done", 0, 0), ("y_first", 3, 0), ("merge_core", 2, 0),
    ("y_second", 3, 0), ("cross", 3, "d"), ("cross", 3, "y"), ("cross", 3, "u"), ("x_done", 1, 0),
    ("x_relay", 2, 0), ("y_opposite", 3, 0), ("cross", 3, "o"), ("merge_core", 3, 0), ("rden", 0, 0),
    ("z_done", 0, 0), ("x_done", 2, 0), ("x_relay", 3, 0), ("spread", 0, 0), ("z_done", 1, 0),
    ("x_done", 3, 0), ("z_done", 2, 0), ("spread_far", 0, 0), ("spread", 1, 0), ("z_done", 3, 0),
    ("contract", 0, 0), ("spread_far", 1, 0), ("spread", 2, 0), ("spread", 3, 0), ("contract", 1, 0),
    ("spread_far", 2, 0), ("spread_far", 3, 0), ("contract", 2, 0), ("contract", 3, 0),
)


def kernel(
    ints, amp, fock, eps_occ, eps_vir, out,
    gath, ampv, fockv, acc, temp, rden, done, occs, virs,
    give, take, part, x1s, x1r, x2s, x2r, zs, zr, dres,
    in_sem, out_sem, send_sem, ra, raz, rcore, rx1, rx2, rz, rd,
):
    vir = ints.shape[1]
    half = vir // 2
    x, zh, p = lax.axis_index("x"), lax.axis_index("zh"), lax.axis_index("core")
    y, zl = lax.axis_index("y"), lax.axis_index("zl")
    side = zl // 2
    m = zl + side * (3 - 2 * zl)
    dz = 1 - 2 * side
    rows = [v + side * (3 - 2 * v) for v in (m, 1 - m, 2, 3)]
    yu, yd, yo = lax.rem(y + 1, 4), lax.rem(y + 3, 4), lax.rem(y + 2, 4)
    xu, xd, xo = lax.rem(x + 1, 4), lax.rem(x + 3, 4), lax.rem(x + 2, 4)
    of_y = {"y": y, "u": yu, "d": yd, "o": yo}
    me = dict(x=x, zh=zh, core=p, y=y, zl=zl)

    def at(**where):
        there = {**me, **where}
        return tuple(there[name] for name in ("x", "zh", "core", "y", "zl"))

    z_plus, z_minus = at(zl=zl + dz), at(zl=zl - dz)
    y_up, y_down = at(y=yu), at(y=yd)
    x_up, x_down = at(x=xu), at(x=xd)
    z_far, mate = at(zh=1 - zh), at(core=1 - p)

    started = []

    def send(src, dst, sem, where, guard=None):
        copy = pltpu.make_async_remote_copy(
            src_ref=src, dst_ref=dst, send_sem=send_sem.at[len(started)],
            recv_sem=sem, device_id=where, device_id_type=MESH,
        )
        if guard is None:
            copy.start()
        else:
            pl.when(guard)(copy.start)
        started.append((copy, guard))

    def arrived(dst, sem):
        pltpu.make_async_remote_copy(
            src_ref=dst, dst_ref=dst, send_sem=send_sem.at[0],
            recv_sem=sem, device_id=mate, device_id_type=MESH,
        ).wait_recv()

    own = pltpu.make_async_copy(ints, gath.at[rows[0], y], in_sem.at[0])
    own.start()
    loads = [
        pltpu.make_async_copy(amp.at[:, pl.ds(0, half)], ampv.at[0], in_sem.at[1]),
        pltpu.make_async_copy(amp.at[:, pl.ds(half, half)], ampv.at[1], in_sem.at[2]),
        pltpu.make_async_copy(fock, fockv, in_sem.at[3]),
        pltpu.make_async_copy(eps_occ, occs, in_sem.at[4]),
        pltpu.make_async_copy(eps_vir, virs, in_sem.at[5]),
    ]
    for load in loads:
        load.start()

    barrier = pltpu.get_barrier_semaphore()
    for where in (z_plus, y_up, y_down, x_up, x_down, z_far, mate):
        pl.semaphore_signal(barrier, inc=1, device_id=where, device_id_type=MESH)

    @pl.when(m == 1)
    def _():
        pl.semaphore_signal(barrier, inc=1, device_id=z_minus, device_id_type=MESH)

    own.wait()
    pl.semaphore_wait(barrier, 7 + m)

    lo, hi = pl.ds(0, half), pl.ds(half, half)
    is_mine = x * 4 + zh * 2 + p == y * 4 + zl

    def span(i, table=CHUNKS):
        return table[i][1], table[i][2]

    def cut(i, table=CHUNKS):
        a, b = span(i, table)
        middle = a + ((b - a) // 16 + i % 2) // 2 * 16
        return pl.ds(a, middle - a), pl.ds(middle, b - middle)

    def whole(i, table=CHUNKS):
        a, b = span(i, table)
        return pl.ds(a, b - a)

    def block(i, q):
        return gath.at[rows[CHUNKS[i][0]], q, whole(i)]

    def send_y(i):
        b, s = block(i, y), ra.at[i, y]
        send(b.at[:, lo], b.at[:, lo], s.at[0], y_up)
        send(b.at[:, hi], b.at[:, hi], s.at[1], y_down)
        send(b.at[:, hi], b.at[:, hi], s.at[1], y_up)
        send(b.at[:, lo], b.at[:, lo], s.at[0], y_down)

    def start_own():
        b, s = gath.at[rows[0], y], raz.at[rows[0]]
        send(b, b, s, z_plus)
        send(b, b, s, z_minus, m == 1)
        for i, chunk in enumerate(CHUNKS):
            if chunk[0] == 0:
                send_y(i)

    def z_forward(k):
        b, s = gath.at[rows[k], y], raz.at[rows[k]]
        pl.when(m == 1)(lambda: arrived(b, s))
        send(b, b, s, z_plus if k == 1 else z_minus, m == 1)

    def z_arrive(k):
        b, s = gath.at[rows[k], y], raz.at[rows[k]]
        pl.when(m == 0)(lambda: arrived(b, s))

    def y_first(i):
        b, s = block(i, yd), ra.at[i, yd, 0]
        arrived(b.at[:, lo], s)
        send(b.at[:, lo], b.at[:, lo], s, y_up)
        b, s = block(i, yu), ra.at[i, yu, 1]
        arrived(b.at[:, hi], s)
        send(b.at[:, hi], b.at[:, hi], s, y_down)

    def y_second(i):
        arrived(block(i, yd).at[:, hi], ra.at[i, yd, 1])
        arrived(block(i, yu).at[:, lo], ra.at[i, yu, 0])

    def y_opposite(i):
        arrived(block(i, yo).at[:, lo], ra.at[i, yo, 0])
        arrived(block(i, yo).at[:, hi], ra.at[i, yo, 1])

    def cross(i, which):
        k, (a, b), q = CHUNKS[i][0], span(i), of_y[which]
        left = gath.at[rows[k], q, whole(i)]

        def term(into, h):
            into[...] = jnp.dot(left[...], ampv[h], preferred_element_type=F32)
            for side_of in range(2):

                @pl.when(is_mine & (h == side_of))
                def _(side_of=side_of):
                    into[...] += left[:, side_of * half : (side_of + 1) * half].astype(F32)

        term(temp.at[pl.ds(0, b - a)], 1 - p)
        give[k, q, a:b] = temp[: b - a].astype(BF)
        sent = (k, q, whole(i))
        send(give.at[sent], take.at[sent], rcore.at[i, q], mate)
        term(part.at[k, q, whole(i)], p)

    def merge_core(i):
        k, (a, b) = CHUNKS[i][0], span(i)
        for q in (y, yd, yu, yo):
            arrived(take.at[k, q, whole(i)], rcore.at[i, q])
        x1s[k, a:b] = (part[k, xo, a:b] + take[k, xo, a:b].astype(F32)).astype(BF)
        head, tail = cut(i)
        send(x1s.at[k, head], x1r.at[k, head], rx1.at[i, 0], x_up)
        send(x1s.at[k, tail], x1r.at[k, tail], rx1.at[i, 1], x_down)
        for q in (xu, xd, x):
            part[k, q, a:b] += take[k, q, a:b].astype(F32)

    def x_relay(i):
        k, (a, b) = CHUNKS[i][0], span(i)
        head, tail = cut(i)
        arrived(x1r.at[k, head], rx1.at[i, 0])
        x2s[k, 0, head] = (part[k, xu, head] + x1r[k, head].astype(F32)).astype(BF)
        x2s[k, 0, tail] = part[k, xu, tail].astype(BF)
        send(x2s.at[k, 0, whole(i)], x2r.at[k, 0, whole(i)], rx2.at[i, 0], x_up)
        arrived(x1r.at[k, tail], rx1.at[i, 1])
        x2s[k, 1, head] = part[k, xd, head].astype(BF)
        x2s[k, 1, tail] = (part[k, xd, tail] + x1r[k, tail].astype(F32)).astype(BF)
        send(x2s.at[k, 1, whole(i)], x2r.at[k, 1, whole(i)], rx2.at[i, 1], x_down)

    def x_done(i):
        k, (a, b) = CHUNKS[i][0], span(i)
        arrived(x2r.at[k, 0, whole(i)], rx2.at[i, 0])
        arrived(x2r.at[k, 1, whole(i)], rx2.at[i, 1])
        both = x2r[k, 0, a:b].astype(F32) + x2r[k, 1, a:b].astype(F32)
        zs[k, a:b] = (part[k, x, a:b] + both).astype(BF)
        for c, (of, first, last) in enumerate(PIECES):
            if of == k and a <= first and last <= b:
                r = whole(c, PIECES)
                send(zs.at[k, r], zr.at[k, r], rz.at[c], z_far)

    def z_done(i):
        k, (a, b) = PIECES[i][0], span(i, PIECES)
        arrived(zr.at[k, whole(i, PIECES)], rz.at[i])
        dres[k, p, x, a:b] = (zs[k, a:b].astype(F32) + zr[k, a:b].astype(F32)).astype(BF)
        b, s = dres.at[k, p, x, whole(i, PIECES)], rd.at[i, p, x]
        send(b, b, s.at[0], x_up)
        send(b, b, s.at[0], x_down)
        send(b, b, s.at[0], mate)

    def spread(i):
        k = PIECES[i][0]
        head, tail = cut(i, PIECES)
        for q, piece, sem, where in ((xd, head, 0, x_up), (xu, tail, 1, x_down)):
            b, s = dres.at[k, p, q, whole(i, PIECES)], rd.at[i, p, q]
            arrived(b, s.at[0])
            c = dres.at[k, p, q, piece]
            send(c, c, s.at[sem], where)
            send(b, b, s.at[0], mate)

    def spread_far(i):
        k = PIECES[i][0]
        head, tail = cut(i, PIECES)
        arrived(dres.at[k, p, xo, head], rd.at[i, p, xo, 0])
        arrived(dres.at[k, p, xo, tail], rd.at[i, p, xo, 1])
        b = dres.at[k, p, xo, whole(i, PIECES)]
        send(b, b, rd.at[i, p, xo, 0], mate)

    def put(h):
        return pltpu.make_async_copy(
            done.at[pl.ds(h * half, half)], out.at[pl.ds(h * half, half)], out_sem.at[h]
        )

    def contract(i):
        k, (a, b) = PIECES[i][0], span(i, PIECES)
        for q in (x, xd, xu, xo):
            arrived(dres.at[k, 1 - p, q, whole(i, PIECES)], rd.at[i, 1 - p, q, 0])
        left = gath[rows[k], :, a:b].reshape(4 * (b - a), vir)
        right = jnp.concatenate(
            [dres[k, h, :, a:b].reshape(4 * (b - a), half) for h in range(2)], axis=-1
        )
        last = ORDER[-1] == ("contract", i, 0)
        for h in range(2):
            r = slice(h * half, (h + 1) * half)
            term = lax.dot_general(
                left[:, r], right, (((0,), (0,)), ((), ())), preferred_element_type=F32
            )
            if last:
                change = (acc[r] + term) * rden[r]
                for c in range(2):
                    cols = slice(c * half, (c + 1) * half)
                    done[r, cols] = (ampv[c, r].astype(F32) - change[:, cols]).astype(BF)
                put(h).start()
            else:
                acc[r] += term

    def load_wait():
        for load in loads:
            load.wait()

    def fock_term():
        acc[...] = jnp.dot(ampv[0], fockv[:half], preferred_element_type=F32) + jnp.dot(
            ampv[1], fockv[half:], preferred_element_type=F32
        )

    def denominators():
        level = occs[x * 4 + zh * 2 + p]
        level2 = occs[y * 4 + zl]
        across = virs[...].reshape(1, vir)
        down = jnp.broadcast_to(across, (128, vir)).T[:, :1]
        rden[...] = 1.0 / (((down + across) - level) - level2)

    for name, i, which in ORDER:
        if name == "cross":
            cross(i, which)
        elif name == "start_own":
            start_own()
        elif name == "load_wait":
            load_wait()
        elif name == "fock":
            fock_term()
        elif name == "rden":
            denominators()
        else:
            {
                "z_arrive": z_arrive, "z_forward": z_forward, "send_y": send_y, "y_first": y_first,
                "y_second": y_second, "y_opposite": y_opposite, "merge_core": merge_core,
                "x_relay": x_relay, "x_done": x_done, "z_done": z_done, "spread": spread,
                "spread_far": spread_far, "contract": contract,
            }[name](i)

    for copy, guard in started:
        if guard is None:
            copy.wait_send()
        else:
            pl.when(guard)(copy.wait_send)
    for h in range(2):
        put(h).wait()


def local(amplitudes, ints, eps_occ, eps_vir, fock_vir):
    vir, depth = ints.shape[1], ints.shape[2]
    half = vir // 2
    n, n2 = len(CHUNKS), len(PIECES)
    anywhere = pl.BlockSpec(memory_space=pl.ANY)
    dma = pltpu.SemaphoreType.DMA
    updated = pl.pallas_call(
        kernel,
        out_shape=jax.ShapeDtypeStruct((vir, vir), BF),
        in_specs=[anywhere] * 5,
        out_specs=anywhere,
        scratch_shapes=[
            pltpu.VMEM((4, 4, depth, vir), BF),
            pltpu.VMEM((2, vir, half), BF),
            pltpu.VMEM((vir, vir), BF),
            pltpu.VMEM((vir, vir), F32),
            pltpu.VMEM((depth, half), F32),
            pltpu.VMEM((vir, vir), F32),
            pltpu.VMEM((vir, vir), BF),
            pltpu.SMEM(eps_occ.shape, F32),
            pltpu.VMEM((vir,), F32),
            pltpu.VMEM((4, 4, depth, half), BF),
            pltpu.VMEM((4, 4, depth, half), BF),
            pltpu.VMEM((4, 4, depth, half), F32),
            pltpu.VMEM((4, depth, half), BF),
            pltpu.VMEM((4, depth, half), BF),
            pltpu.VMEM((4, 2, depth, half), BF),
            pltpu.VMEM((4, 2, depth, half), BF),
            pltpu.VMEM((4, depth, half), BF),
            pltpu.VMEM((4, depth, half), BF),
            pltpu.VMEM((4, 2, 4, depth, half), BF),
            dma((6,)), dma((2,)), dma((5 + 14 * n + 9 * n2,)),
            dma((n, 4, 2)), dma((4,)), dma((n, 4)), dma((n, 2)), dma((n, 2)),
            dma((n2,)), dma((n2, 2, 4, 2)),
        ],
        compiler_params=pltpu.CompilerParams(
            collective_id=0, has_side_effects=True, vmem_limit_bytes=60 * 1024 * 1024
        ),
        name="doubles_update",
    )(ints[0].T, amplitudes[0, 0], fock_vir, eps_occ, eps_vir)
    return updated[None, None]


def solution(mesh):
    torus = Mesh(mesh.devices.reshape(4, 2, 2, 4, 4), ("x", "zh", "core", "y", "zl"))
    placed = (P(ROW, COL, None, None), P(ROW, None, COL), P(), P(), P())
    return jax.shard_map(
        local, mesh=torus, in_specs=placed, out_specs=P(ROW, COL, None, None), check_vma=False
    )
```

```python
import jax
import jax.numpy as jnp
from jax import lax
from jax.experimental import pallas as pl
from jax.experimental.pallas import tpu as pltpu
from jax.sharding import Mesh
from jax.sharding import PartitionSpec as P

COL = ("y", "zl")
ROW = ("x", "zh", "core")
MESH = pl.DeviceIdType.MESH
BF = jnp.bfloat16
F32 = jnp.float32

CHUNKS = (
    (0, 0, 144), (1, 0, 144), (2, 0, 144), (3, 0, 144),
)
PIECES = (
    (0, 0, 144), (1, 0, 144), (2, 0, 144), (3, 0, 64), (3, 64, 144),
)
ORDER = (
    ("start_own", 0, 0), ("y_first", 0, 0), ("z_forward", 1, 0), ("z_arrive", 1, 0), ("send_y", 1, 0),
    ("z_forward", 2, 0), ("y_second", 0, 0), ("load_wait", 0, 0), ("cross", 0, "y"), ("cross", 0, "u"),
    ("cross", 0, "d"), ("z_forward", 3, 0), ("y_opposite", 0, 0), ("cross", 1, "y"), ("cross", 0, "o"),
    ("y_first", 1, 0), ("z_arrive", 2, 0), ("send_y", 2, 0), ("merge_core", 0, 0), ("y_second", 1, 0),
    ("cross", 1, "u"), ("fock", 0, 0), ("cross", 1, "d"), ("x_relay", 0, 0), ("y_opposite", 1, 0),
    ("cross", 1, "o"), ("y_first", 2, 0), ("merge_core", 1, 0), ("cross", 2, "y"), ("x_done", 0, 0),
    ("z_arrive", 3, 0), ("send_y", 3, 0), ("cross", 3, "y"), ("y_second", 2, 0), ("cross", 2, "d"),
    ("rden", 0, 0), ("cross", 2, "u"), ("x_relay", 1, 0), ("y_opposite", 2, 0), ("cross", 2, "o"),
    ("merge_core", 2, 0), ("y_first", 3, 0), ("z_done", 0, 0), ("x_done", 1, 0), ("y_second", 3, 0),
    ("x_relay", 2, 0), ("cross", 3, "d"), ("cross", 3, "u"), ("y_opposite", 3, 0), ("cross", 3, "o"),
    ("merge_core", 3, 0), ("x_done", 2, 0), ("spread", 0, 0), ("x_relay", 3, 0), ("spread_far", 0, 0),
    ("z_done", 1, 0), ("x_done", 3, 0), ("z_done", 2, 0), ("spread", 1, 0), ("contract", 0, 0),
    ("spread", 2, 0), ("z_done", 3, 0), ("z_done", 4, 0), ("spread_far", 1, 0), ("spread", 3, 0),
    ("spread_far", 2, 0), ("spread", 4, 0), ("contract", 1, 0), ("spread_far", 3, 0), ("contract", 4, 1),
    ("spread_far", 4, 0), ("contract", 2, 0), ("contract", 3, 0), ("contract", 4, 2),
)


def kernel(
    ints, amp, fock, eps_occ, eps_vir, out,
    gath, ampv, fockv, acc, temp, rden, done, occs, virs,
    give, take, part, x1s, x1r, x2s, x2r, zs, zr, dres,
    in_sem, out_sem, send_sem, ra, raz, rcore, rx1, rx2, rz, rd,
):
    vir = ints.shape[1]
    half = vir // 2
    x, zh, p = lax.axis_index("x"), lax.axis_index("zh"), lax.axis_index("core")
    y, zl = lax.axis_index("y"), lax.axis_index("zl")
    side = zl // 2
    m = zl + side * (3 - 2 * zl)
    dz = 1 - 2 * side
    rows = [v + side * (3 - 2 * v) for v in (m, 1 - m, 2, 3)]
    yu, yd, yo = lax.rem(y + 1, 4), lax.rem(y + 3, 4), lax.rem(y + 2, 4)
    xu, xd, xo = lax.rem(x + 1, 4), lax.rem(x + 3, 4), lax.rem(x + 2, 4)
    of_y = {"y": y, "u": yu, "d": yd, "o": yo}
    me = dict(x=x, zh=zh, core=p, y=y, zl=zl)

    def at(**where):
        there = {**me, **where}
        return tuple(there[name] for name in ("x", "zh", "core", "y", "zl"))

    z_plus, z_minus = at(zl=zl + dz), at(zl=zl - dz)
    y_up, y_down = at(y=yu), at(y=yd)
    x_up, x_down = at(x=xu), at(x=xd)
    z_far, mate = at(zh=1 - zh), at(core=1 - p)

    started = []

    def send(src, dst, sem, where, guard=None):
        copy = pltpu.make_async_remote_copy(
            src_ref=src, dst_ref=dst, send_sem=send_sem.at[len(started)],
            recv_sem=sem, device_id=where, device_id_type=MESH,
        )
        if guard is None:
            copy.start()
        else:
            pl.when(guard)(copy.start)
        started.append((copy, guard))

    def arrived(dst, sem):
        pltpu.make_async_remote_copy(
            src_ref=dst, dst_ref=dst, send_sem=send_sem.at[0],
            recv_sem=sem, device_id=mate, device_id_type=MESH,
        ).wait_recv()

    own = pltpu.make_async_copy(ints, gath.at[rows[0], y], in_sem.at[0])
    own.start()
    loads = [
        pltpu.make_async_copy(amp.at[:, pl.ds(0, half)], ampv.at[0], in_sem.at[1]),
        pltpu.make_async_copy(amp.at[:, pl.ds(half, half)], ampv.at[1], in_sem.at[2]),
        pltpu.make_async_copy(fock, fockv, in_sem.at[3]),
        pltpu.make_async_copy(eps_occ, occs, in_sem.at[4]),
        pltpu.make_async_copy(eps_vir, virs, in_sem.at[5]),
    ]
    for load in loads:
        load.start()

    barrier = pltpu.get_barrier_semaphore()
    for where in (z_plus, y_up, y_down, x_up, x_down, z_far, mate):
        pl.semaphore_signal(barrier, inc=1, device_id=where, device_id_type=MESH)

    @pl.when(m == 1)
    def _():
        pl.semaphore_signal(barrier, inc=1, device_id=z_minus, device_id_type=MESH)

    own.wait()
    pl.semaphore_wait(barrier, 7 + m)

    lo, hi = pl.ds(0, half), pl.ds(half, half)
    is_mine = x * 4 + zh * 2 + p == y * 4 + zl

    def span(i, table=CHUNKS):
        return table[i][1], table[i][2]

    def cut(i, table=CHUNKS):
        a, b = span(i, table)
        middle = a + ((b - a) // 16 + i % 2) // 2 * 16
        return pl.ds(a, middle - a), pl.ds(middle, b - middle)

    def whole(i, table=CHUNKS):
        a, b = span(i, table)
        return pl.ds(a, b - a)

    def block(i, q):
        return gath.at[rows[CHUNKS[i][0]], q, whole(i)]

    def send_y(i):
        b, s = block(i, y), ra.at[i, y]
        send(b.at[:, lo], b.at[:, lo], s.at[0], y_up)
        send(b.at[:, hi], b.at[:, hi], s.at[1], y_down)
        send(b.at[:, hi], b.at[:, hi], s.at[1], y_up)
        send(b.at[:, lo], b.at[:, lo], s.at[0], y_down)

    def start_own():
        b, s = gath.at[rows[0], y], raz.at[rows[0]]
        send(b, b, s, z_plus)
        send(b, b, s, z_minus, m == 1)
        for i, chunk in enumerate(CHUNKS):
            if chunk[0] == 0:
                send_y(i)

    def z_forward(k):
        b, s = gath.at[rows[k], y], raz.at[rows[k]]
        pl.when(m == 1)(lambda: arrived(b, s))
        send(b, b, s, z_plus if k == 1 else z_minus, m == 1)

    def z_arrive(k):
        b, s = gath.at[rows[k], y], raz.at[rows[k]]
        pl.when(m == 0)(lambda: arrived(b, s))

    def y_first(i):
        b, s = block(i, yd), ra.at[i, yd, 0]
        arrived(b.at[:, lo], s)
        send(b.at[:, lo], b.at[:, lo], s, y_up)
        b, s = block(i, yu), ra.at[i, yu, 1]
        arrived(b.at[:, hi], s)
        send(b.at[:, hi], b.at[:, hi], s, y_down)

    def y_second(i):
        arrived(block(i, yd).at[:, hi], ra.at[i, yd, 1])
        arrived(block(i, yu).at[:, lo], ra.at[i, yu, 0])

    def y_opposite(i):
        arrived(block(i, yo).at[:, lo], ra.at[i, yo, 0])
        arrived(block(i, yo).at[:, hi], ra.at[i, yo, 1])

    def cross(i, which):
        k, (a, b), q = CHUNKS[i][0], span(i), of_y[which]
        left = gath.at[rows[k], q, whole(i)]

        def term(into, h):
            into[...] = jnp.dot(left[...], ampv[h], preferred_element_type=F32)
            for side_of in range(2):

                @pl.when(is_mine & (h == side_of))
                def _(side_of=side_of):
                    into[...] += left[:, side_of * half : (side_of + 1) * half].astype(F32)

        term(temp.at[pl.ds(0, b - a)], 1 - p)
        give[k, q, a:b] = temp[: b - a].astype(BF)
        sent = (k, q, whole(i))
        send(give.at[sent], take.at[sent], rcore.at[i, q], mate)
        term(part.at[k, q, whole(i)], p)

    def merge_core(i):
        k, (a, b) = CHUNKS[i][0], span(i)
        for q in (y, yd, yu, yo):
            arrived(take.at[k, q, whole(i)], rcore.at[i, q])
        x1s[k, a:b] = (part[k, xo, a:b] + take[k, xo, a:b].astype(F32)).astype(BF)
        head, tail = cut(i)
        send(x1s.at[k, head], x1r.at[k, head], rx1.at[i, 0], x_up)
        send(x1s.at[k, tail], x1r.at[k, tail], rx1.at[i, 1], x_down)
        for q in (xu, xd, x):
            part[k, q, a:b] += take[k, q, a:b].astype(F32)

    def x_relay(i):
        k, (a, b) = CHUNKS[i][0], span(i)
        head, tail = cut(i)
        arrived(x1r.at[k, head], rx1.at[i, 0])
        x2s[k, 0, head] = (part[k, xu, head] + x1r[k, head].astype(F32)).astype(BF)
        x2s[k, 0, tail] = part[k, xu, tail].astype(BF)
        send(x2s.at[k, 0, whole(i)], x2r.at[k, 0, whole(i)], rx2.at[i, 0], x_up)
        arrived(x1r.at[k, tail], rx1.at[i, 1])
        x2s[k, 1, head] = part[k, xd, head].astype(BF)
        x2s[k, 1, tail] = (part[k, xd, tail] + x1r[k, tail].astype(F32)).astype(BF)
        send(x2s.at[k, 1, whole(i)], x2r.at[k, 1, whole(i)], rx2.at[i, 1], x_down)

    def x_done(i):
        k, (a, b) = CHUNKS[i][0], span(i)
        arrived(x2r.at[k, 0, whole(i)], rx2.at[i, 0])
        arrived(x2r.at[k, 1, whole(i)], rx2.at[i, 1])
        both = x2r[k, 0, a:b].astype(F32) + x2r[k, 1, a:b].astype(F32)
        zs[k, a:b] = (part[k, x, a:b] + both).astype(BF)
        for c, (of, first, last) in enumerate(PIECES):
            if of == k and a <= first and last <= b:
                r = whole(c, PIECES)
                send(zs.at[k, r], zr.at[k, r], rz.at[c], z_far)

    def z_done(i):
        k, (a, b) = PIECES[i][0], span(i, PIECES)
        arrived(zr.at[k, whole(i, PIECES)], rz.at[i])
        dres[k, p, x, a:b] = (zs[k, a:b].astype(F32) + zr[k, a:b].astype(F32)).astype(BF)
        b, s = dres.at[k, p, x, whole(i, PIECES)], rd.at[i, p, x]
        send(b, b, s.at[0], x_up)
        send(b, b, s.at[0], x_down)
        send(b, b, s.at[0], mate)

    def spread(i):
        k = PIECES[i][0]
        head, tail = cut(i, PIECES)
        for q, piece, sem, where in ((xd, head, 0, x_up), (xu, tail, 1, x_down)):
            b, s = dres.at[k, p, q, whole(i, PIECES)], rd.at[i, p, q]
            arrived(b, s.at[0])
            c = dres.at[k, p, q, piece]
            send(c, c, s.at[sem], where)
            send(b, b, s.at[0], mate)

    def spread_far(i):
        k = PIECES[i][0]
        head, tail = cut(i, PIECES)
        arrived(dres.at[k, p, xo, head], rd.at[i, p, xo, 0])
        arrived(dres.at[k, p, xo, tail], rd.at[i, p, xo, 1])
        b = dres.at[k, p, xo, whole(i, PIECES)]
        send(b, b, rd.at[i, p, xo, 0], mate)

    def put(h):
        return pltpu.make_async_copy(
            done.at[pl.ds(h * half, half)], out.at[pl.ds(h * half, half)], out_sem.at[h]
        )

    def contract(i, part):
        k, (a, b) = PIECES[i][0], span(i, PIECES)
        order = ((x, xd, xu, xo), (x, xd, xu), (xo,))[part]
        for q in order:
            arrived(dres.at[k, 1 - p, q, whole(i, PIECES)], rd.at[i, 1 - p, q, 0])
        if part == 0:
            left = gath[rows[k], :, a:b].reshape(4 * (b - a), vir)
            sides = [dres[k, h, :, a:b].reshape(4 * (b - a), half) for h in range(2)]
        else:
            left = jnp.concatenate([gath[rows[k], q, a:b] for q in order], axis=0)
            sides = [
                jnp.concatenate([dres[k, h, q, a:b] for q in order], axis=0) for h in range(2)
            ]
        right = jnp.concatenate(sides, axis=-1)
        last = ORDER[-1] == ("contract", i, part)
        for h in range(2):
            r = slice(h * half, (h + 1) * half)
            term = lax.dot_general(
                left[:, r], right, (((0,), (0,)), ((), ())), preferred_element_type=F32
            )
            if last:
                change = (acc[r] + term) * rden[r]
                for c in range(2):
                    cols = slice(c * half, (c + 1) * half)
                    done[r, cols] = (ampv[c, r].astype(F32) - change[:, cols]).astype(BF)
                put(h).start()
            else:
                acc[r] += term

    def load_wait():
        for load in loads:
            load.wait()

    def fock_term():
        acc[...] = jnp.dot(ampv[0], fockv[:half], preferred_element_type=F32) + jnp.dot(
            ampv[1], fockv[half:], preferred_element_type=F32
        )

    def denominators():
        level = occs[x * 4 + zh * 2 + p]
        level2 = occs[y * 4 + zl]
        across = virs[...].reshape(1, vir)
        down = jnp.broadcast_to(across, (128, vir)).T[:, :1]
        rden[...] = 1.0 / (((down + across) - level) - level2)

    for name, i, which in ORDER:
        if name == "cross":
            cross(i, which)
        elif name == "contract":
            contract(i, which)
        elif name == "start_own":
            start_own()
        elif name == "load_wait":
            load_wait()
        elif name == "fock":
            fock_term()
        elif name == "rden":
            denominators()
        else:
            {
                "z_arrive": z_arrive, "z_forward": z_forward, "send_y": send_y, "y_first": y_first,
                "y_second": y_second, "y_opposite": y_opposite, "merge_core": merge_core,
                "x_relay": x_relay, "x_done": x_done, "z_done": z_done, "spread": spread,
                "spread_far": spread_far,
            }[name](i)

    for copy, guard in started:
        if guard is None:
            copy.wait_send()
        else:
            pl.when(guard)(copy.wait_send)
    for h in range(2):
        put(h).wait()


def local(amplitudes, ints, eps_occ, eps_vir, fock_vir):
    vir, depth = ints.shape[1], ints.shape[2]
    half = vir // 2
    n, n2 = len(CHUNKS), len(PIECES)
    anywhere = pl.BlockSpec(memory_space=pl.ANY)
    dma = pltpu.SemaphoreType.DMA
    updated = pl.pallas_call(
        kernel,
        out_shape=jax.ShapeDtypeStruct((vir, vir), BF),
        in_specs=[anywhere] * 5,
        out_specs=anywhere,
        scratch_shapes=[
            pltpu.VMEM((4, 4, depth, vir), BF),
            pltpu.VMEM((2, vir, half), BF),
            pltpu.VMEM((vir, vir), BF),
            pltpu.VMEM((vir, vir), F32),
            pltpu.VMEM((depth, half), F32),
            pltpu.VMEM((vir, vir), F32),
            pltpu.VMEM((vir, vir), BF),
            pltpu.SMEM(eps_occ.shape, F32),
            pltpu.VMEM((vir,), F32),
            pltpu.VMEM((4, 4, depth, half), BF),
            pltpu.VMEM((4, 4, depth, half), BF),
            pltpu.VMEM((4, 4, depth, half), F32),
            pltpu.VMEM((4, depth, half), BF),
            pltpu.VMEM((4, depth, half), BF),
            pltpu.VMEM((4, 2, depth, half), BF),
            pltpu.VMEM((4, 2, depth, half), BF),
            pltpu.VMEM((4, depth, half), BF),
            pltpu.VMEM((4, depth, half), BF),
            pltpu.VMEM((4, 2, 4, depth, half), BF),
            dma((6,)), dma((2,)), dma((5 + 14 * n + 9 * n2,)),
            dma((n, 4, 2)), dma((4,)), dma((n, 4)), dma((n, 2)), dma((n, 2)),
            dma((n2,)), dma((n2, 2, 4, 2)),
        ],
        compiler_params=pltpu.CompilerParams(
            collective_id=0, has_side_effects=True, vmem_limit_bytes=60 * 1024 * 1024
        ),
        name="doubles_update",
    )(ints[0].T, amplitudes[0, 0], fock_vir, eps_occ, eps_vir)
    return updated[None, None]


def solution(mesh):
    torus = Mesh(mesh.devices.reshape(4, 2, 2, 4, 4), ("x", "zh", "core", "y", "zl"))
    placed = (P(ROW, COL, None, None), P(ROW, None, COL), P(), P(), P())
    return jax.shard_map(
        local, mesh=torus, in_specs=placed, out_specs=P(ROW, COL, None, None), check_vma=False
    )
```

```python
import jax
import jax.numpy as jnp
from jax import lax
from jax.experimental import pallas as pl
from jax.experimental.pallas import tpu as pltpu
from jax.sharding import Mesh
from jax.sharding import PartitionSpec as P

COL = ("y", "zl")
ROW = ("x", "zh", "core")
MESH = pl.DeviceIdType.MESH
BF = jnp.bfloat16
F32 = jnp.float32

CHUNKS = (
    (0, 0, 144), (1, 0, 144), (2, 0, 144), (3, 0, 144),
)
PIECES = (
    (0, 0, 144), (1, 0, 144), (2, 0, 144), (3, 0, 64), (3, 64, 144),
)
ORDER = (
    ("start_own", 0, 0), ("y_first", 0, 0), ("z_forward", 1, 0), ("z_arrive", 1, 0), ("send_y", 1, 0),
    ("z_forward", 2, 0), ("y_second", 0, 0), ("load_wait", 0, 0), ("cross", 0, "y"), ("cross", 0, "u"),
    ("cross", 0, "d"), ("z_forward", 3, 0), ("y_opposite", 0, 0), ("cross", 1, "y"), ("cross", 0, "o"),
    ("y_first", 1, 0), ("z_arrive", 2, 0), ("send_y", 2, 0), ("merge_core", 0, 0), ("y_second", 1, 0),
    ("cross", 1, "u"), ("fock", 0, 0), ("cross", 1, "d"), ("x_relay", 0, 0), ("y_opposite", 1, 0),
    ("cross", 1, "o"), ("y_first", 2, 0), ("merge_core", 1, 0), ("cross", 2, "y"), ("x_done", 0, 0),
    ("z_arrive", 3, 0), ("send_y", 3, 0), ("cross", 3, "y"), ("y_second", 2, 0), ("cross", 2, "d"),
    ("rden", 0, 0), ("cross", 2, "u"), ("x_relay", 1, 0), ("y_opposite", 2, 0), ("cross", 2, "o"),
    ("merge_core", 2, 0), ("y_first", 3, 0), ("z_done", 0, 0), ("x_done", 1, 0), ("y_second", 3, 0),
    ("x_relay", 2, 0), ("cross", 3, "d"), ("cross", 3, "u"), ("y_opposite", 3, 0), ("cross", 3, "o"),
    ("merge_core", 3, 0), ("x_done", 2, 0), ("spread", 0, 0), ("x_relay", 3, 0), ("spread_far", 0, 0),
    ("z_done", 1, 0), ("x_done", 3, 0), ("z_done", 2, 0), ("spread", 1, 0), ("contract", 0, 0),
    ("spread", 2, 0), ("z_done", 3, 0), ("z_done", 4, 0), ("spread_far", 1, 0), ("spread", 3, 0),
    ("spread_far", 2, 0), ("spread", 4, 0), ("contract", 1, 0), ("spread_far", 3, 0), ("contract", 4, 1),
    ("spread_far", 4, 0), ("contract", 2, 0), ("contract", 3, 0), ("contract", 4, 2),
)


def kernel(
    ints, amp, fock, eps_occ, eps_vir, out,
    gath, ampv, fockv, acc, temp, rden, done, occs, virs,
    give, take, part, x1s, x1r, x2s, x2r, zs, zr, dres,
    in_sem, out_sem, send_sem, ra, raz, rcore, rx1, rx2, rz, rd,
):
    vir = ints.shape[1]
    half, third = vir // 2, vir // 3
    x, zh, p = lax.axis_index("x"), lax.axis_index("zh"), lax.axis_index("core")
    y, zl = lax.axis_index("y"), lax.axis_index("zl")
    side = zl // 2
    m = zl + side * (3 - 2 * zl)
    dz = 1 - 2 * side
    rows = [v + side * (3 - 2 * v) for v in (m, 1 - m, 2, 3)]
    yu, yd, yo = lax.rem(y + 1, 4), lax.rem(y + 3, 4), lax.rem(y + 2, 4)
    xu, xd, xo = lax.rem(x + 1, 4), lax.rem(x + 3, 4), lax.rem(x + 2, 4)
    of_y = {"y": y, "u": yu, "d": yd, "o": yo}
    me = dict(x=x, zh=zh, core=p, y=y, zl=zl)

    def at(**where):
        there = {**me, **where}
        return tuple(there[name] for name in ("x", "zh", "core", "y", "zl"))

    z_plus, z_minus = at(zl=zl + dz), at(zl=zl - dz)
    y_up, y_down = at(y=yu), at(y=yd)
    x_up, x_down = at(x=xu), at(x=xd)
    z_far, mate = at(zh=1 - zh), at(core=1 - p)

    started = []

    def send(src, dst, sem, where, guard=None):
        copy = pltpu.make_async_remote_copy(
            src_ref=src, dst_ref=dst, send_sem=send_sem.at[len(started)],
            recv_sem=sem, device_id=where, device_id_type=MESH,
        )
        if guard is None:
            copy.start()
        else:
            pl.when(guard)(copy.start)
        started.append((copy, guard))

    def arrived(dst, sem):
        pltpu.make_async_remote_copy(
            src_ref=dst, dst_ref=dst, send_sem=send_sem.at[0],
            recv_sem=sem, device_id=mate, device_id_type=MESH,
        ).wait_recv()

    own = pltpu.make_async_copy(ints, gath.at[rows[0], y], in_sem.at[0])
    own.start()
    loads = [
        pltpu.make_async_copy(amp.at[:, pl.ds(0, half)], ampv.at[0], in_sem.at[1]),
        pltpu.make_async_copy(amp.at[:, pl.ds(half, half)], ampv.at[1], in_sem.at[2]),
        pltpu.make_async_copy(fock, fockv, in_sem.at[3]),
        pltpu.make_async_copy(eps_occ, occs, in_sem.at[4]),
        pltpu.make_async_copy(eps_vir, virs, in_sem.at[5]),
    ]
    for load in loads:
        load.start()

    barrier = pltpu.get_barrier_semaphore()
    for where in (z_plus, y_up, y_down, x_up, x_down, z_far, mate):
        pl.semaphore_signal(barrier, inc=1, device_id=where, device_id_type=MESH)

    @pl.when(m == 1)
    def _():
        pl.semaphore_signal(barrier, inc=1, device_id=z_minus, device_id_type=MESH)

    own.wait()
    pl.semaphore_wait(barrier, 7 + m)

    lo, hi = pl.ds(0, half), pl.ds(half, half)
    is_mine = x * 4 + zh * 2 + p == y * 4 + zl

    def span(i, table=CHUNKS):
        return table[i][1], table[i][2]

    def cut(i, table=CHUNKS):
        a, b = span(i, table)
        middle = a + ((b - a) // 16 + i % 2) // 2 * 16
        return pl.ds(a, middle - a), pl.ds(middle, b - middle)

    def whole(i, table=CHUNKS):
        a, b = span(i, table)
        return pl.ds(a, b - a)

    def block(i, q):
        return gath.at[rows[CHUNKS[i][0]], q, whole(i)]

    def send_y(i):
        b, s = block(i, y), ra.at[i, y]
        send(b.at[:, lo], b.at[:, lo], s.at[0], y_up)
        send(b.at[:, hi], b.at[:, hi], s.at[1], y_down)
        send(b.at[:, hi], b.at[:, hi], s.at[1], y_up)
        send(b.at[:, lo], b.at[:, lo], s.at[0], y_down)

    def start_own():
        b, s = gath.at[rows[0], y], raz.at[rows[0]]
        send(b, b, s, z_plus)
        send(b, b, s, z_minus, m == 1)
        for i, chunk in enumerate(CHUNKS):
            if chunk[0] == 0:
                send_y(i)

    def z_forward(k):
        b, s = gath.at[rows[k], y], raz.at[rows[k]]
        pl.when(m == 1)(lambda: arrived(b, s))
        send(b, b, s, z_plus if k == 1 else z_minus, m == 1)

    def z_arrive(k):
        b, s = gath.at[rows[k], y], raz.at[rows[k]]
        pl.when(m == 0)(lambda: arrived(b, s))

    def y_first(i):
        b, s = block(i, yd), ra.at[i, yd, 0]
        arrived(b.at[:, lo], s)
        send(b.at[:, lo], b.at[:, lo], s, y_up)
        b, s = block(i, yu), ra.at[i, yu, 1]
        arrived(b.at[:, hi], s)
        send(b.at[:, hi], b.at[:, hi], s, y_down)

    def y_second(i):
        arrived(block(i, yd).at[:, hi], ra.at[i, yd, 1])
        arrived(block(i, yu).at[:, lo], ra.at[i, yu, 0])

    def y_opposite(i):
        arrived(block(i, yo).at[:, lo], ra.at[i, yo, 0])
        arrived(block(i, yo).at[:, hi], ra.at[i, yo, 1])

    def cross(i, which):
        k, (a, b), q = CHUNKS[i][0], span(i), of_y[which]
        left = gath.at[rows[k], q, whole(i)]

        def term(into, h):
            into[...] = jnp.dot(left[...], ampv[h], preferred_element_type=F32)
            for side_of in range(2):

                @pl.when(is_mine & (h == side_of))
                def _(side_of=side_of):
                    into[...] += left[:, side_of * half : (side_of + 1) * half].astype(F32)

        term(temp.at[pl.ds(0, b - a)], 1 - p)
        give[k, q, a:b] = temp[: b - a].astype(BF)
        sent = (k, q, whole(i))
        send(give.at[sent], take.at[sent], rcore.at[i, q], mate)
        term(part.at[k, q, whole(i)], p)

    def merge_core(i):
        k, (a, b) = CHUNKS[i][0], span(i)
        for q in (y, yd, yu, yo):
            arrived(take.at[k, q, whole(i)], rcore.at[i, q])
        x1s[k, a:b] = (part[k, xo, a:b] + take[k, xo, a:b].astype(F32)).astype(BF)
        head, tail = cut(i)
        send(x1s.at[k, head], x1r.at[k, head], rx1.at[i, 0], x_up)
        send(x1s.at[k, tail], x1r.at[k, tail], rx1.at[i, 1], x_down)
        for q in (xu, xd, x):
            part[k, q, a:b] += take[k, q, a:b].astype(F32)

    def x_relay(i):
        k, (a, b) = CHUNKS[i][0], span(i)
        head, tail = cut(i)
        arrived(x1r.at[k, head], rx1.at[i, 0])
        x2s[k, 0, head] = (part[k, xu, head] + x1r[k, head].astype(F32)).astype(BF)
        x2s[k, 0, tail] = part[k, xu, tail].astype(BF)
        send(x2s.at[k, 0, whole(i)], x2r.at[k, 0, whole(i)], rx2.at[i, 0], x_up)
        arrived(x1r.at[k, tail], rx1.at[i, 1])
        x2s[k, 1, head] = part[k, xd, head].astype(BF)
        x2s[k, 1, tail] = (part[k, xd, tail] + x1r[k, tail].astype(F32)).astype(BF)
        send(x2s.at[k, 1, whole(i)], x2r.at[k, 1, whole(i)], rx2.at[i, 1], x_down)

    def x_done(i):
        k, (a, b) = CHUNKS[i][0], span(i)
        arrived(x2r.at[k, 0, whole(i)], rx2.at[i, 0])
        arrived(x2r.at[k, 1, whole(i)], rx2.at[i, 1])
        both = x2r[k, 0, a:b].astype(F32) + x2r[k, 1, a:b].astype(F32)
        zs[k, a:b] = (part[k, x, a:b] + both).astype(BF)
        for c, (of, first, last) in enumerate(PIECES):
            if of == k and a <= first and last <= b:
                r = whole(c, PIECES)
                send(zs.at[k, r], zr.at[k, r], rz.at[c], z_far)

    def z_done(i):
        k, (a, b) = PIECES[i][0], span(i, PIECES)
        arrived(zr.at[k, whole(i, PIECES)], rz.at[i])
        dres[k, p, x, a:b] = (zs[k, a:b].astype(F32) + zr[k, a:b].astype(F32)).astype(BF)
        b, s = dres.at[k, p, x, whole(i, PIECES)], rd.at[i, p, x]
        send(b, b, s.at[0], x_up)
        send(b, b, s.at[0], x_down)
        send(b, b, s.at[0], mate)

    def spread(i):
        k = PIECES[i][0]
        head, tail = cut(i, PIECES)
        for q, piece, sem, where in ((xd, head, 0, x_up), (xu, tail, 1, x_down)):
            b, s = dres.at[k, p, q, whole(i, PIECES)], rd.at[i, p, q]
            arrived(b, s.at[0])
            c = dres.at[k, p, q, piece]
            send(c, c, s.at[sem], where)
            send(b, b, s.at[0], mate)

    def spread_far(i):
        k = PIECES[i][0]
        head, tail = cut(i, PIECES)
        arrived(dres.at[k, p, xo, head], rd.at[i, p, xo, 0])
        arrived(dres.at[k, p, xo, tail], rd.at[i, p, xo, 1])
        b = dres.at[k, p, xo, whole(i, PIECES)]
        send(b, b, rd.at[i, p, xo, 0], mate)

    def put(h):
        return pltpu.make_async_copy(
            done.at[pl.ds(h * third, third)], out.at[pl.ds(h * third, third)], out_sem.at[h]
        )

    def contract(i, part):
        k, (a, b) = PIECES[i][0], span(i, PIECES)
        order = ((x, xd, xu, xo), (x, xd, xu), (xo,))[part]
        for q in order:
            arrived(dres.at[k, 1 - p, q, whole(i, PIECES)], rd.at[i, 1 - p, q, 0])
        if part == 0:
            left = gath[rows[k], :, a:b].reshape(4 * (b - a), vir)
            sides = [dres[k, h, :, a:b].reshape(4 * (b - a), half) for h in range(2)]
        else:
            left = jnp.concatenate([gath[rows[k], q, a:b] for q in order], axis=0)
            sides = [
                jnp.concatenate([dres[k, h, q, a:b] for q in order], axis=0) for h in range(2)
            ]
        right = jnp.concatenate(sides, axis=-1)
        last = ORDER[-1] == ("contract", i, part)
        for h in range(3):
            r = slice(h * third, (h + 1) * third)
            term = lax.dot_general(
                left[:, r], right, (((0,), (0,)), ((), ())), preferred_element_type=F32
            )
            if last:
                change = (acc[r] + term) * rden[r]
                for c in range(2):
                    cols = slice(c * half, (c + 1) * half)
                    done[r, cols] = (ampv[c, r].astype(F32) - change[:, cols]).astype(BF)
                put(h).start()
            else:
                acc[r] += term

    def load_wait():
        for load in loads:
            load.wait()

    def fock_term():
        acc[...] = jnp.dot(ampv[0], fockv[:half], preferred_element_type=F32) + jnp.dot(
            ampv[1], fockv[half:], preferred_element_type=F32
        )

    def denominators():
        level = occs[x * 4 + zh * 2 + p]
        level2 = occs[y * 4 + zl]
        across = virs[...].reshape(1, vir)
        down = jnp.broadcast_to(across, (128, vir)).T[:, :1]
        rden[...] = 1.0 / (((down + across) - level) - level2)

    for name, i, which in ORDER:
        if name == "cross":
            cross(i, which)
        elif name == "contract":
            contract(i, which)
        elif name == "start_own":
            start_own()
        elif name == "load_wait":
            load_wait()
        elif name == "fock":
            fock_term()
        elif name == "rden":
            denominators()
        else:
            {
                "z_arrive": z_arrive, "z_forward": z_forward, "send_y": send_y, "y_first": y_first,
                "y_second": y_second, "y_opposite": y_opposite, "merge_core": merge_core,
                "x_relay": x_relay, "x_done": x_done, "z_done": z_done, "spread": spread,
                "spread_far": spread_far,
            }[name](i)

    for copy, guard in started:
        if guard is None:
            copy.wait_send()
        else:
            pl.when(guard)(copy.wait_send)
    for h in range(3):
        put(h).wait()


def local(amplitudes, ints, eps_occ, eps_vir, fock_vir):
    vir, depth = ints.shape[1], ints.shape[2]
    half = vir // 2
    n, n2 = len(CHUNKS), len(PIECES)
    anywhere = pl.BlockSpec(memory_space=pl.ANY)
    dma = pltpu.SemaphoreType.DMA
    updated = pl.pallas_call(
        kernel,
        out_shape=jax.ShapeDtypeStruct((vir, vir), BF),
        in_specs=[anywhere] * 5,
        out_specs=anywhere,
        scratch_shapes=[
            pltpu.VMEM((4, 4, depth, vir), BF),
            pltpu.VMEM((2, vir, half), BF),
            pltpu.VMEM((vir, vir), BF),
            pltpu.VMEM((vir, vir), F32),
            pltpu.VMEM((depth, half), F32),
            pltpu.VMEM((vir, vir), F32),
            pltpu.VMEM((vir, vir), BF),
            pltpu.SMEM(eps_occ.shape, F32),
            pltpu.VMEM((vir,), F32),
            pltpu.VMEM((4, 4, depth, half), BF),
            pltpu.VMEM((4, 4, depth, half), BF),
            pltpu.VMEM((4, 4, depth, half), F32),
            pltpu.VMEM((4, depth, half), BF),
            pltpu.VMEM((4, depth, half), BF),
            pltpu.VMEM((4, 2, depth, half), BF),
            pltpu.VMEM((4, 2, depth, half), BF),
            pltpu.VMEM((4, depth, half), BF),
            pltpu.VMEM((4, depth, half), BF),
            pltpu.VMEM((4, 2, 4, depth, half), BF),
            dma((6,)), dma((3,)), dma((5 + 14 * n + 9 * n2,)),
            dma((n, 4, 2)), dma((4,)), dma((n, 4)), dma((n, 2)), dma((n, 2)),
            dma((n2,)), dma((n2, 2, 4, 2)),
        ],
        compiler_params=pltpu.CompilerParams(
            collective_id=0, has_side_effects=True, vmem_limit_bytes=60 * 1024 * 1024
        ),
        name="doubles_update",
    )(ints[0].T, amplitudes[0, 0], fock_vir, eps_occ, eps_vir)
    return updated[None, None]


def solution(mesh):
    torus = Mesh(mesh.devices.reshape(4, 2, 2, 4, 4), ("x", "zh", "core", "y", "zl"))
    placed = (P(ROW, COL, None, None), P(ROW, None, COL), P(), P(), P())
    return jax.shard_map(
        local, mesh=torus, in_specs=placed, out_specs=P(ROW, COL, None, None), check_vma=False
    )
```
